32 devices in a mesh: parts: 2 (over x), gx: 4 (over y, core), gy: 4 (over z).
Axes of the slice: x: 2, y: 2, z: 4, core: 2. Of those that a mesh axis runs over, the one named last changes fastest.
Arguments:
- forcing_right_side: float32 [32, 32, 1024], P(('parts', 'gx'), 'gy'), parts along dimension 0, may hold values from -18 to 18
- earlier_warmth: float32 [32, 32, 1024], P(('parts', 'gx'), 'gy'), parts along dimension 0, may hold values from 0 to 2
- matter_condition: int32 [32, 32, 1024], P(('parts', 'gx'), 'gy'), parts along dimension 0, may hold values from 0 to 2
- compressed_slot_number: int32 [32, 32, 1024], P(('parts', 'gx'), 'gy'), parts along dimension 0, may hold values from 0 to 127
- normal_draw_factor: float32 [32, 32, 1024], P(('parts', 'gx'), 'gy'), parts along dimension 0, may hold values from -6 to 6
Outputs:
- solution: float32 [32, 32, 1024], P(('parts', 'gx'), 'gy'), parts along dimension 0
- residual: float32 [32, 32, 1024], P(('parts', 'gx'), 'gy'), parts along dimension 0
The draws below stay inside these ranges and needn't reach their ends.
There are 2 independent parts, one for each index of `parts`. The reference program is written for one: setup_inputs(seed, part) draws one part's arguments, and reference() takes and returns one part's arrays. A program takes and returns all parts, laid end to end along the dimension named above; each array names one. Nothing has to cross between parts.
Inputs may be any that keep to these rules, and one draw needn't show every extreme that they name: `matter_condition`: phase labels the cell as powder, solid or liquid. `compressed_slot_number`: each cell's row of the sketch.
All inputs are finite; a program needn't handle non-finite values.
Results may differ from the reference program's by a relative error of at most 0.0003.
Values sent between devices are 32-bit elements; how exact they have to be, the bound alone decides.
A program may use at most 64 MiB of HBM per device.

```python
import jax
import jax.numpy as jnp
from jax import lax

MESH_SPAN_UPWARD = 1024
BASIS = 2
CYCLES = 1
SKETCH = 128
MESH_SPAN_EAST = 16
MESH_SPAN_NORTH = 32


def set_ends(entries, rng, low, largest):
    place = [jax.random.randint(jax.random.fold_in(rng, axis), (), 0, length) for axis, length in enumerate(entries.shape)]
    widest = entries.shape.index(max(entries.shape))
    next_to = place[:widest] + [(place[widest] + 1) % entries.shape[widest]] + place[widest + 1:]
    return entries.at[tuple(place)].set(low).at[tuple(next_to)].set(largest)


def steps_of(key, dims, shards, low, top_value):
    factor_of, own = 1.0, jax.random.fold_in(key, 6)
    for axis_at, blocks in shards:
        steps = jnp.exp(jax.random.uniform(jax.random.fold_in(own, axis_at), (blocks,), jnp.float32, low / len(shards), top_value / len(shards)))
        factor_of = factor_of * jnp.repeat(steps, dims[axis_at] // blocks).reshape([-1 if axis == axis_at else 1 for axis in range(len(dims))])
    return factor_of


def gaussian(rng, dims, spread, limit, shards=(), kind=jnp.bfloat16):
    factor_of = steps_of(rng, dims, shards, -0.22, 0.18) if shards else 1.0
    entries = jax.random.normal(rng, dims, jnp.float32) * spread * factor_of
    return jnp.minimum(jnp.maximum(entries, -limit), limit).astype(kind)


def setup_inputs(seed: int = 0, part: int = 0) -> dict:
    key_list = jax.random.split(jax.random.key(seed), 6)
    part_splits = jax.random.split(jax.random.fold_in(key_list[5], part), 6)
    forcing_right_side = gaussian(part_splits[0], (MESH_SPAN_EAST, MESH_SPAN_NORTH, MESH_SPAN_UPWARD), 3.0, 18.0, ((0, 4), (1, 4)), jnp.float32)
    earlier_warmth = jnp.clip(2.0 * jax.random.uniform(part_splits[1], (MESH_SPAN_EAST, MESH_SPAN_NORTH, MESH_SPAN_UPWARD), jnp.float32) ** steps_of(part_splits[1], (MESH_SPAN_EAST, MESH_SPAN_NORTH, MESH_SPAN_UPWARD), ((0, 4), (1, 4)), -0.2, 0.2), 0.0, 2.0)
    matter_condition = set_ends(jax.random.randint(part_splits[2], (MESH_SPAN_EAST, MESH_SPAN_NORTH, MESH_SPAN_UPWARD), 0, 3), jax.random.fold_in(part_splits[2], 1), 0, 2).astype(jnp.int32)
    compressed_slot_number = set_ends(jax.random.randint(part_splits[3], (MESH_SPAN_EAST, MESH_SPAN_NORTH, MESH_SPAN_UPWARD), 0, SKETCH), jax.random.fold_in(part_splits[3], 1), 0, SKETCH - 1).astype(jnp.int32)
    normal_draw_factor = gaussian(part_splits[4], (MESH_SPAN_EAST, MESH_SPAN_NORTH, MESH_SPAN_UPWARD), 1.0, 6.0, ((0, 4), (1, 4)), jnp.float32)
    return {"forcing_right_side": forcing_right_side, "earlier_warmth": earlier_warmth, "matter_condition": matter_condition, "compressed_slot_number": compressed_slot_number, "normal_draw_factor": normal_draw_factor}


epsilon = 1e-06
highest = lax.Precision.HIGHEST

def medium_traits(earlier_warmth, matter_condition):
    datum_offset = jnp.where(matter_condition == 0, 0.2, jnp.where(matter_condition == 1, 1.0, 0.6)).astype(jnp.float32)
    spreading_rate = datum_offset * (0.5 + earlier_warmth)
    volumetric_retention = jnp.where(matter_condition == 0, 1.0, jnp.where(matter_condition == 1, 2.0, 1.5)).astype(jnp.float32)
    return (spreading_rate, volumetric_retention)

def harmonic(first, second):
    return 2.0 * first * second / (first + second)

def shifted(field):
    padded = jnp.pad(field, 1)
    return [padded[2:, 1:-1, 1:-1], padded[:-2, 1:-1, 1:-1], padded[1:-1, 2:, 1:-1], padded[1:-1, :-2, 1:-1], padded[1:-1, 1:-1, 2:], padded[1:-1, 1:-1, :-2]]

def operate(field, volumetric_retention, links):
    result = volumetric_retention * field
    for conductance, neighbour in zip(links, shifted(field)):
        result = result + conductance * (field - neighbour)
    return result

def solve_small(hess, scale_norm):
    width_count = hess.shape[1]
    gram_matrix = jnp.dot(hess.T, hess, precision=highest)
    target = scale_norm * hess[0]
    factor = jnp.linalg.cholesky(gram_matrix)
    forward = []
    for row_a in range(width_count):
        partial_sum = target[row_a]
        for prior in range(row_a):
            partial_sum = partial_sum - factor[row_a, prior] * forward[prior]
        forward.append(partial_sum / factor[row_a, row_a])
    backward = [None] * width_count
    for row_a in reversed(range(width_count)):
        partial_sum = forward[row_a]
        for later in range(row_a + 1, width_count):
            partial_sum = partial_sum - factor[later, row_a] * backward[later]
        backward[row_a] = partial_sum / factor[row_a, row_a]
    return backward

def reference(forcing_right_side, earlier_warmth, matter_condition, compressed_slot_number, normal_draw_factor):
    spreading_rate, volumetric_retention = medium_traits(earlier_warmth, matter_condition)
    links = [harmonic(spreading_rate, other) for other in shifted(spreading_rate)]

    def sketch_of(field):
        return jax.ops.segment_sum((normal_draw_factor * field).reshape(-1), compressed_slot_number.reshape(-1), num_segments=SKETCH)
    solution = jnp.zeros_like(forcing_right_side)
    residual = forcing_right_side
    for cycle_number in range(CYCLES):
        if cycle_number > 0:
            residual = forcing_right_side - operate(solution, volumetric_retention, links)
        sketched = sketch_of(residual)
        scale_norm = jnp.sqrt(jnp.sum(sketched * sketched) + epsilon)
        basis_list = [residual / scale_norm]
        sketch_list = [sketched / scale_norm]
        columns = []
        for column in range(BASIS):
            images = operate(basis_list[column], volumetric_retention, links)
            image_sketch = sketch_of(images)
            stacked = jnp.stack(sketch_list, axis=1)
            coeffs = jnp.dot(stacked.T, image_sketch, precision=highest)
            reduced = images
            for prior in range(column + 1):
                reduced = reduced - coeffs[prior] * basis_list[prior]
            remainder = sketch_of(reduced)
            norm_next = jnp.sqrt(jnp.sum(remainder * remainder) + epsilon)
            columns.append(jnp.concatenate([coeffs, norm_next[None], jnp.zeros((BASIS - column - 1,), coeffs.dtype)]))
            if column + 1 < BASIS:
                basis_list.append(reduced / norm_next)
                sketch_list.append(remainder / norm_next)
        hess = jnp.stack(columns, axis=1)
        weights = solve_small(hess, scale_norm)
        for prior in range(BASIS):
            solution = solution + weights[prior] * basis_list[prior]
    residual = forcing_right_side - operate(solution, volumetric_retention, links)
    return (solution, residual)
```

```python
import functools

import jax
import jax.numpy as jnp
from jax import lax
from jax.experimental import pallas as pl
from jax.experimental.pallas import tpu as pltpu
from jax.sharding import PartitionSpec as P

SKETCH = 128
LOW = 16
HIGH = SKETCH // LOW
MESH = pl.DeviceIdType.MESH
epsilon = 1e-06
highest = lax.Precision.HIGHEST
f32 = jnp.float32
bf16 = jnp.bfloat16


def harmonic(first, second):
    return 2.0 * first * second / (first + second)


def total(field):
    return jnp.sum(jnp.sum(field, axis=1, keepdims=True), axis=0, keepdims=True)


def coefficients(s0, s1, s2):
    beta2 = total(s0 * s0) + epsilon
    h00 = total(s0 * s1) / beta2
    t0 = s1 - h00 * s0
    w1 = s2 - h00 * s1
    n0sq = total(t0 * t0) / beta2 + epsilon
    in_q0 = total(s0 * w1) / beta2
    h11 = total(t0 * w1) / (beta2 * n0sq)
    n0 = jnp.sqrt(n0sq)
    h01 = in_q0 / n0
    t1 = w1 - in_q0 * s0 - h11 * t0
    n1sq = total(t1 * t1) / (beta2 * n0sq) + epsilon
    m00 = h00 * h00 + n0sq
    m01 = h00 * h01 + n0 * h11
    m11 = h01 * h01 + h11 * h11 + n1sq
    l00 = jnp.sqrt(m00)
    l10 = m01 / l00
    l11 = jnp.sqrt(m11 - l10 * l10)
    f0 = h00 / l00
    f1 = (h01 - l10 * f0) / l11
    y1 = f1 / l11
    y0 = (f0 - l10 * y1) / l00
    c1 = y1 / n0
    c0 = y0 - c1 * h00
    return c0, c1


def kernel(
    ngx, ngy, nx, ny, nz,
    f_hbm, w_hbm, m_hbm, s_hbm, d_hbm,
    answer, rest,
    z1, z2, r, w, m, slot, d, cond, diag, lx, ly, lydown, lz, lzleft, lyb, onehot, parts, wedge, sedge,
    hx_r, hx_c, hx_z, hx_s, hx_d, hy_rc, hy_z, hy_s, hy_d, py_rc, py_z, py_s, py_d,
    mine, gathered, load_sem, hs_sem, hr_sem, as_sem, ar_sem, known,
):
    gx = lax.axis_index("gx")
    gy = lax.axis_index("gy")
    count = ngx * ngy
    me = gx * ngy + gy


    def peer(step):
        other = lax.rem(me + step, count)
        return {"gx": lax.div(other, ngy), "gy": lax.rem(other, ngy)}

    barrier = pltpu.get_barrier_semaphore()

    for step in range(1, ngx):
        other = {"gx": lax.rem(gx + step, ngx), "gy": gy}
        pl.semaphore_signal(barrier, inc=1, device_id=other, device_id_type=MESH)

    has_x = (gx > 0, gx < ngx - 1)
    has_y = (gy > 0, gy < ngy - 1)
    to_x = ({"gx": gx - 1, "gy": gy}, {"gx": gx + 1, "gy": gy})
    to_y = ({"gx": gx, "gy": gy - 1}, {"gx": gx, "gy": gy + 1})
    for s in (0, 1):

        @pl.when(has_y[s])
        def _():
            pl.semaphore_signal(barrier, inc=1, device_id=to_y[s], device_id_type=MESH)

    loads = [
        pltpu.make_async_copy(src, dst, load_sem.at[i])
        for i, (src, dst) in enumerate(
            ((w_hbm, w), (m_hbm, m), (f_hbm, r), (s_hbm, slot), (d_hbm, d))
        )
    ]
    for load in loads:
        load.start()

    def tell(turn):
        for s in (0, 1):

            @pl.when(has_y[s])
            def _():
                pl.semaphore_signal(known.at[turn, 1 - s], inc=1, device_id=to_y[s], device_id_type=MESH)

    def hear(turn):
        for s in (0, 1):

            @pl.when(has_y[s])
            def _():
                pl.semaphore_wait(known.at[turn, s], 1)

    edge_x = (0, nx - 1)
    edge_y = (0, ny - 1)

    def remote(src, dst, index, side, target):
        return pltpu.make_async_remote_copy(
            src_ref=src,
            dst_ref=dst.at[1 - side],
            send_sem=hs_sem.at[index, side],
            recv_sem=hr_sem.at[index, 1 - side],
            device_id=target,
            device_id_type=MESH,
        )

    def x_copies(src, dst, index):
        return [(has_x[s], remote(src.at[edge_x[s]], dst, index, s, to_x[s])) for s in (0, 1)]

    def y_copies(src, dst, index):
        return [(has_y[s], remote(src.at[s], dst, index, s, to_y[s])) for s in (0, 1)]

    def begin(copies):
        for there, copy in copies:
            pl.when(there)(copy.start)

    def arrive(copies):
        for there, copy in copies:
            pl.when(there)(copy.wait_send)

    def recv_wait(dst, index, side, src, there, target):
        copy = pltpu.make_async_remote_copy(
            src_ref=src,
            dst_ref=dst.at[side],
            send_sem=hs_sem.at[index, side],
            recv_sem=hr_sem.at[index, side],
            device_id=target,
            device_id_type=MESH,
        )
        pl.when(there)(copy.wait_recv)

    loads[0].wait()
    loads[1].wait()
    for x in range(nx):
        phase = m[x]
        cond[x] = jnp.where(phase == 0, 0.2, jnp.where(phase == 1, 1.0, 0.6)).astype(f32) * (0.5 + w[x])
    loads[2].wait()
    for s in (0, 1):
        for x in range(nx):
            py_rc[s, pl.ds(x, 1), :] = r[x, pl.ds(edge_y[s], 1), :]
            py_rc[s, pl.ds(nx + x, 1), :] = cond[x, pl.ds(edge_y[s], 1), :]

        @pl.when(jnp.logical_not(has_x[s]))
        def _():
            hx_r[s] = jnp.zeros((ny, nz), f32)
            hx_c[s] = jnp.zeros((ny, nz), f32)
            hx_z[s] = jnp.zeros((ny, nz), f32)
            hx_d[s] = jnp.zeros((ny, nz), f32)
            hx_s[s] = jnp.zeros((ny, nz), jnp.int32)

        @pl.when(jnp.logical_not(has_y[s]))
        def _():
            hy_rc[s] = jnp.zeros((2 * nx, nz), f32)
            hy_z[s] = jnp.zeros((nx, nz), f32)
            hy_d[s] = jnp.zeros((nx, nz), f32)
            hy_s[s] = jnp.zeros((nx, nz), jnp.int32)

    pl.semaphore_wait(barrier, ngx - 1 + has_y[0].astype(jnp.int32) + has_y[1].astype(jnp.int32))
    first = x_copies(cond, hx_c, 0) + y_copies(py_rc, hy_rc, 1) + x_copies(r, hx_r, 2)
    begin(first)
    if ngy > 1:
        tell(1)
    loads[3].wait()
    loads[4].wait()
    for s in (0, 1):
        for x in range(nx):
            py_s[s, pl.ds(x, 1), :] = slot[x, pl.ds(edge_y[s], 1), :]
            py_d[s, pl.ds(x, 1), :] = d[x, pl.ds(edge_y[s], 1), :]
    early = x_copies(slot, hx_s, 5) + y_copies(py_s, hy_s, 6) + x_copies(d, hx_d, 7) + y_copies(py_d, hy_d, 8)
    begin(early)

    lane = lax.broadcasted_iota(jnp.int32, (ny, nz), 1)
    row = lax.broadcasted_iota(jnp.int32, (ny, nz), 0)
    row_high = lax.broadcasted_iota(jnp.int32, (HIGH, nz), 0)
    row_low = lax.broadcasted_iota(jnp.int32, (LOW, nz), 0)

    def spread(ref, y, rows):
        return jnp.broadcast_to(ref[pl.ds(y, 1), :], (rows, nz))

    def low_rows(slots, y):
        low = jnp.bitwise_and(spread(slots, y, LOW), LOW - 1)
        return jnp.where(low == row_low, 1.0, 0.0).astype(bf16)

    def add_row(sums, slots, fields, right, y):
        mask = lax.shift_right_logical(spread(slots, y, HIGH), 4) == row_high
        left = jnp.concatenate([jnp.where(mask, spread(field, y, HIGH), 0.0) for field in fields], axis=0)
        return sums + lax.dot_general(
            left.astype(bf16), right, (((1,), (1,)), ((), ())), preferred_element_type=f32
        )

    def split(high, low, weighted):
        upper = weighted.astype(bf16).astype(f32)
        high[...] = upper
        low[...] = weighted - upper

    for x in range(nx):
        here = cond[x]
        if x > 0:
            lx[x] = harmonic(cond[x - 1], here)
        right = jnp.where(lane == nz - 1, 0.0, harmonic(here, pltpu.roll(here, nz - 1, 1)))
        up = jnp.where(row == ny - 1, 0.0, harmonic(here, pltpu.roll(here, ny - 1, 0)))
        lz[x] = right
        lzleft[x] = pltpu.roll(right, 1, 1)
        ly[x] = up
        lydown[x] = pltpu.roll(up, 1, 0)
    for x in range(nx):
        phase = m[x]
        cap = jnp.where(phase == 0, 1.0, jnp.where(phase == 1, 2.0, 1.5)).astype(f32)
        whole = cap + lz[x] + lzleft[x] + ly[x] + lydown[x]
        if x > 0:
            whole = whole + lx[x]
        if x < nx - 1:
            whole = whole + lx[x + 1]
        diag[x] = whole

    def apply(field, x):
        v = field[x]
        out = diag[x] * v
        if x > 0:
            out = out - lx[x] * field[x - 1]
        if x < nx - 1:
            out = out - lx[x + 1] * field[x + 1]
        out = out - ly[x] * pltpu.roll(v, ny - 1, 0) - lydown[x] * pltpu.roll(v, 1, 0)
        return out - lz[x] * pltpu.roll(v, nz - 1, 1) - lzleft[x] * pltpu.roll(v, 1, 1)

    for x in range(nx):
        z1[x] = apply(r, x)

    def begin_sketch(x, sums):
        split(parts.at[0, x], parts.at[1, x], d[x] * r[x])
        for y in range(ny):
            right = low_rows(slot.at[x], y)
            onehot[x, y] = right
            sums = add_row(sums, slot.at[x], (parts.at[0, x], parts.at[1, x]), right, y)
        return sums

    sums = lax.fori_loop(0, nx, begin_sketch, jnp.zeros((2 * HIGH, LOW), f32))
    mine[...] = jnp.zeros((HIGH, SKETCH), f32)
    mine[:, 0:LOW] = sums[:HIGH] + sums[HIGH:]
    for turn in range(2, ngy):
        hear(turn - 1)
        tell(turn)

    for s in (0, 1):
        recv_wait(hx_c, 0, s, cond.at[0], has_x[s], to_x[s])
        recv_wait(hy_rc, 1, s, py_rc.at[0], has_y[s], to_y[s])
        recv_wait(hx_r, 2, s, r.at[0], has_x[s], to_x[s])
    for s in (0, 1):
        e = edge_x[s]
        link = harmonic(hx_c[s], cond[e])
        lx[nx * s] = link
        z1[e] = z1[e] + link * (r[e] - hx_r[s])
    for s in (0, 1):
        for x in range(nx):
            link = harmonic(hy_rc[s, pl.ds(nx + x, 1), :], py_rc[s, pl.ds(nx + x, 1), :])
            lyb[s, pl.ds(x, 1), :] = link
            flux = link * (py_rc[s, pl.ds(x, 1), :] - hy_rc[s, pl.ds(x, 1), :])
            after = z1[x, pl.ds(edge_y[s], 1), :] + flux
            z1[x, pl.ds(edge_y[s], 1), :] = after
            py_z[s, pl.ds(x, 1), :] = after
    second = x_copies(z1, hx_z, 3) + y_copies(py_z, hy_z, 4)
    begin(second)
    for x in range(nx):
        out = apply(z1, x)
        for s in (0, 1):
            if x == edge_x[s]:
                out = out + lx[nx * s] * z1[x]
        z2[x] = out
        for s in (0, 1):
            at = (x, pl.ds(edge_y[s], 1), slice(None))
            z2[at] = z2[at] + lyb[s, pl.ds(x, 1), :] * py_z[s, pl.ds(x, 1), :]
    sums = jnp.zeros((4 * HIGH, LOW), f32)
    for x in range(nx):
        split(parts.at[0, x], parts.at[1, x], d[x] * z1[x])
        split(parts.at[2, x], parts.at[3, x], d[x] * z2[x])
        for y in range(ny):
            sums = add_row(sums, slot.at[x], [parts.at[k, x] for k in range(4)], onehot[x, y], y)
    for s in (0, 1):
        recv_wait(hx_s, 5, s, slot.at[0], has_x[s], to_x[s])
        recv_wait(hy_s, 6, s, py_s.at[0], has_y[s], to_y[s])
        recv_wait(hx_d, 7, s, d.at[0], has_x[s], to_x[s])
        recv_wait(hy_d, 8, s, py_d.at[0], has_y[s], to_y[s])
    edge_sums = jnp.zeros((2 * HIGH, LOW), f32)
    for s in (0, 1):
        split(wedge.at[0, s], wedge.at[1, s], -lx[nx * s] * z1[edge_x[s]] * hx_d[s])
        for x in range(nx):
            at = pl.ds(s * nx + x, 1)
            edge = -lyb[s, pl.ds(x, 1), :] * py_z[s, pl.ds(x, 1), :] * hy_d[s, pl.ds(x, 1), :]
            upper = edge.astype(bf16).astype(f32)
            wedge[0, 2, at, :] = upper
            wedge[1, 2, at, :] = edge - upper
            sedge[at, :] = hy_s[s, pl.ds(x, 1), :]
    for t, slots in enumerate((hx_s.at[0], hx_s.at[1], sedge)):
        for y in range(ny if t < 2 else 2 * nx):
            edge_sums = add_row(edge_sums, slots, (wedge.at[0, t], wedge.at[1, t]), low_rows(slots, y), y)
    mine[:, LOW : 2 * LOW] = sums[:HIGH] + sums[HIGH : 2 * HIGH]
    mine[:, 2 * LOW : 3 * LOW] = (
        sums[2 * HIGH : 3 * HIGH] + sums[3 * HIGH :] + edge_sums[:HIGH] + edge_sums[HIGH:]
    )

    def share(step, carry):
        pltpu.make_async_remote_copy(
            src_ref=mine,
            dst_ref=gathered.at[me],
            send_sem=as_sem.at[step],
            recv_sem=ar_sem.at[me],
            device_id=peer(step),
            device_id_type=MESH,
        ).start()
        return carry

    if ngy > 1:
        hear(ngy - 1)
    lax.fori_loop(1, count, share, 0)
    gathered[me] = mine[...]
    arrive(first)
    arrive(early)
    arrive(second)
    for s in (0, 1):
        recv_wait(hx_z, 3, s, z1.at[0], has_x[s], to_x[s])
        recv_wait(hy_z, 4, s, py_z.at[0], has_y[s], to_y[s])
        z2[edge_x[s]] = z2[edge_x[s]] - lx[nx * s] * hx_z[s]
        for x in range(nx):
            link = lyb[s, pl.ds(x, 1), :]
            at = (x, pl.ds(edge_y[s], 1), slice(None))
            z2[at] = z2[at] - link * hy_z[s, pl.ds(x, 1), :]

    def collect(step, carry):
        other = lax.rem(me + step, count)
        copy = pltpu.make_async_remote_copy(
            src_ref=mine,
            dst_ref=gathered.at[other],
            send_sem=as_sem.at[step],
            recv_sem=ar_sem.at[other],
            device_id=peer(step),
            device_id_type=MESH,
        )
        copy.wait_recv()
        copy.wait_send()
        return carry

    lax.fori_loop(1, count, collect, 0)
    summed = jnp.sum(gathered[...], axis=0)
    c0, c1 = coefficients(*(summed[:, k * LOW : (k + 1) * LOW] for k in range(3)))
    for x in range(nx):
        answer[x] = c0 * r[x] + c1 * z1[x]
        rest[x] = r[x] - c0 * z1[x] - c1 * z2[x]


def put_out(answer, rest, answer_out, rest_out, sem):
    one = pltpu.make_async_copy(answer, answer_out, sem.at[0])
    two = pltpu.make_async_copy(rest, rest_out, sem.at[1])
    one.start()
    two.start()
    one.wait()
    two.wait()


def body(ngx, ngy, f, w, m, s, d):
    nx, ny, nz = f.shape
    count = ngx * ngy
    vm = lambda shape, dtype=f32: pltpu.VMEM(shape, dtype)
    block = (nx, ny, nz)
    assert 2 * nx <= ny
    answer, rest = pl.pallas_call(
        functools.partial(kernel, ngx, ngy, nx, ny, nz),
        out_shape=(vm(block), vm(block)),
        in_specs=[pl.BlockSpec(memory_space=pl.ANY)] * 5,
        out_specs=[pl.BlockSpec(memory_space=pltpu.VMEM)] * 2,
        scratch_shapes=[
            vm(block), vm(block),
            vm(block), vm(block), vm(block, jnp.int32), vm(block, jnp.int32), vm(block),
            vm(block), vm(block),
            vm((nx + 1, ny, nz)), vm(block), vm(block), vm(block), vm(block), vm((2, nx, nz)),
            vm((nx, ny, LOW, nz), bf16), vm((4, nx, ny, nz)), vm((2, 3, ny, nz)), vm((ny, nz), jnp.int32),
            vm((2, ny, nz)), vm((2, ny, nz)), vm((2, ny, nz)), vm((2, ny, nz), jnp.int32), vm((2, ny, nz)),
            vm((2, 2 * nx, nz)), vm((2, nx, nz)), vm((2, nx, nz), jnp.int32), vm((2, nx, nz)),
            vm((2, 2 * nx, nz)), vm((2, nx, nz)), vm((2, nx, nz), jnp.int32), vm((2, nx, nz)),
            vm((HIGH, SKETCH)), vm((count, HIGH, SKETCH)),
            pltpu.SemaphoreType.DMA((5,)),
            pltpu.SemaphoreType.DMA((9, 2)),
            pltpu.SemaphoreType.DMA((9, 2)),
            pltpu.SemaphoreType.DMA((count,)),
            pltpu.SemaphoreType.DMA((count,)),
            pltpu.SemaphoreType.REGULAR((ngy, 2)),
        ],
        compiler_params=pltpu.CompilerParams(collective_id=0, has_side_effects=True),
        name="sketched_gmres",
    )(f, w, m, s, d)
    return pl.pallas_call(
        put_out,
        out_shape=(jax.ShapeDtypeStruct(block, f32), jax.ShapeDtypeStruct(block, f32)),
        in_specs=[pl.BlockSpec(memory_space=pltpu.VMEM)] * 2,
        out_specs=[pl.BlockSpec(memory_space=pl.ANY)] * 2,
        scratch_shapes=[pltpu.SemaphoreType.DMA((2,))],
        name="put_out",
    )(pltpu.with_memory_space_constraint(answer, pltpu.VMEM), pltpu.with_memory_space_constraint(rest, pltpu.VMEM))


def solution(mesh):
    spec = P(("parts", "gx"), "gy", None)
    return jax.shard_map(
        functools.partial(body, mesh.shape["gx"], mesh.shape["gy"]),
        mesh=mesh,
        in_specs=(spec,) * 5,
        out_specs=(spec, spec),
        check_vma=False,
    )
```

```python
import functools

import jax
import jax.numpy as jnp
from jax import lax
from jax.experimental import pallas as pl
from jax.experimental.pallas import tpu as pltpu
from jax.sharding import PartitionSpec as P

SKETCH = 128
LOW = 16
HIGH = SKETCH // LOW
MESH = pl.DeviceIdType.MESH
epsilon = 1e-06
highest = lax.Precision.HIGHEST
f32 = jnp.float32
bf16 = jnp.bfloat16


def harmonic(first, second):
    return 2.0 * first * second / (first + second)


def total(field):
    return jnp.sum(jnp.sum(field, axis=1, keepdims=True), axis=0, keepdims=True)


def coefficients(s0, s1, s2):
    inv_beta2 = 1.0 / (total(s0 * s0) + epsilon)
    h00 = total(s0 * s1) * inv_beta2
    t0 = s1 - h00 * s0
    w1 = s2 - h00 * s1
    n0sq = total(t0 * t0) * inv_beta2 + epsilon
    cross = total(s0 * w1) * inv_beta2
    inv_n0sq = 1.0 / n0sq
    h11 = total(t0 * w1) * inv_beta2 * inv_n0sq
    t1 = w1 - cross * s0 - h11 * t0
    n1sq = total(t1 * t1) * inv_beta2 * inv_n0sq + epsilon
    minor = h00 * h11 - cross
    inv_det = 1.0 / (minor * minor + n1sq * (h00 * h00 + n0sq))
    return (minor * (h11 + h00) + h00 * n1sq) * inv_det, -minor * inv_det


def kernel(
    ngx, ngy, nx, ny, nz,
    f_hbm, w_hbm, m_hbm, s_hbm, d_hbm,
    answer, rest,
    z1, z2, r, w, m, slot, d, cond, diag, lx, ly, lydown, lz, lzleft, lyb, onehot, parts, wedge, sedge,
    hx_first, hx_early, hx_z, hy_first, hy_early, hy_z,
    px_first, px_early, py_first, py_early, py_z,
    bulk_x, bulk_y, mine, gathered, load_sem, sent, landed, share_sem, known,
):
    gx = lax.axis_index("gx")
    gy = lax.axis_index("gy")
    count = ngx * ngy
    me = gx * ngy + gy


    def peer(step):
        other = lax.rem(me + step, count)
        return {"gx": lax.div(other, ngy), "gy": lax.rem(other, ngy)}

    barrier = pltpu.get_barrier_semaphore()

    for step in range(1, ngx):
        other = {"gx": lax.rem(gx + step, ngx), "gy": gy}
        pl.semaphore_signal(barrier, inc=1, device_id=other, device_id_type=MESH)

    has_x = (gx > 0, gx < ngx - 1)
    has_y = (gy > 0, gy < ngy - 1)
    to_x = ({"gx": gx - 1, "gy": gy}, {"gx": gx + 1, "gy": gy})
    to_y = ({"gx": gx, "gy": gy - 1}, {"gx": gx, "gy": gy + 1})
    for s in (0, 1):

        @pl.when(has_y[s])
        def _():
            pl.semaphore_signal(barrier, inc=1, device_id=to_y[s], device_id_type=MESH)

    loads = [
        pltpu.make_async_copy(src, dst, load_sem.at[i])
        for i, (src, dst) in enumerate(
            ((w_hbm, w), (m_hbm, m), (f_hbm, r), (s_hbm, slot), (d_hbm, d))
        )
    ]
    for load in loads:
        load.start()

    n_y = has_y[0].astype(jnp.int32) + has_y[1].astype(jnp.int32)

    def tell(turn):
        for s in (0, 1):

            @pl.when(has_y[s])
            def _():
                pl.semaphore_signal(known.at[turn - 1], inc=1, device_id=to_y[s], device_id_type=MESH)

    def hear(turn):
        pl.semaphore_wait(known.at[turn - 1], n_y)

    edge_x = (0, nx - 1)
    edge_y = (0, ny - 1)

    def remote(src, dst, axis, index, side, target):
        return pltpu.make_async_remote_copy(
            src_ref=src,
            dst_ref=dst.at[1 - side],
            send_sem=sent.at[axis],
            recv_sem=landed.at[axis, index],
            device_id=target,
            device_id_type=MESH,
        )

    def begin(index, src_x, dst_x, src_y, dst_y):
        for s in (0, 1):
            pl.when(has_x[s])(remote(src_x(s), dst_x, 0, index, s, to_x[s]).start)
        for s in (0, 1):
            pl.when(has_y[s])(remote(src_y(s), dst_y, 1, index, s, to_y[s]).start)

    def settle(axis, has, sem, ref, kind):
        target = to_x[0] if axis == 0 else to_y[0]

        def wait(part):
            copy = pltpu.make_async_remote_copy(
                src_ref=part, dst_ref=part, send_sem=sem, recv_sem=sem, device_id=target, device_id_type=MESH
            )
            return getattr(copy, kind)

        pl.when(jnp.logical_and(has[0], has[1]))(wait(ref))
        pl.when(jnp.logical_xor(has[0], has[1]))(wait(ref.at[0]))

    def arrive(index, dst_x, dst_y):
        settle(0, has_x, landed.at[0, index], dst_x, "wait_recv")
        settle(1, has_y, landed.at[1, index], dst_y, "wait_recv")

    loads[0].wait()
    loads[1].wait()
    for x in range(nx):
        phase = m[x]
        cond[x] = jnp.where(phase == 0, 0.2, jnp.where(phase == 1, 1.0, 0.6)).astype(f32) * (0.5 + w[x])
    loads[2].wait()
    for s in (0, 1):
        e = edge_x[s]
        px_first[s, 0] = cond[e]
        px_first[s, 1] = r[e]
        for x in range(nx):
            py_first[s, pl.ds(x, 1), :] = r[x, pl.ds(edge_y[s], 1), :]
            py_first[s, pl.ds(nx + x, 1), :] = cond[x, pl.ds(edge_y[s], 1), :]

        @pl.when(jnp.logical_not(has_x[s]))
        def _():
            hx_first[s] = jnp.zeros((2, ny, nz), f32)
            hx_early[s] = jnp.zeros((2, ny, nz), f32)
            hx_z[s] = jnp.zeros((ny, nz), f32)

        @pl.when(jnp.logical_not(has_y[s]))
        def _():
            hy_first[s] = jnp.zeros((2 * nx, nz), f32)
            hy_early[s] = jnp.zeros((2 * nx, nz), f32)
            hy_z[s] = jnp.zeros((nx, nz), f32)

    pl.semaphore_wait(barrier, ngx - 1 + n_y)
    begin(0, lambda s: px_first.at[s], hx_first, lambda s: py_first.at[s], hy_first)
    if ngy > 1:
        tell(1)
    loads[3].wait()
    loads[4].wait()
    for s in (0, 1):
        e = edge_x[s]
        px_early[s, 0] = slot[e].astype(f32)
        px_early[s, 1] = d[e]
        for x in range(nx):
            py_early[s, pl.ds(x, 1), :] = slot[x, pl.ds(edge_y[s], 1), :].astype(f32)
            py_early[s, pl.ds(nx + x, 1), :] = d[x, pl.ds(edge_y[s], 1), :]
    begin(1, lambda s: px_early.at[s], hx_early, lambda s: py_early.at[s], hy_early)

    lane = lax.broadcasted_iota(jnp.int32, (ny, nz), 1)
    row = lax.broadcasted_iota(jnp.int32, (ny, nz), 0)
    row_high = lax.broadcasted_iota(jnp.int32, (HIGH, nz), 0)
    row_low = lax.broadcasted_iota(jnp.int32, (LOW, nz), 0)

    def spread(ref, y, rows):
        return jnp.broadcast_to(ref[pl.ds(y, 1), :], (rows, nz))

    def low_rows(slots, y):
        low = jnp.bitwise_and(spread(slots, y, LOW), LOW - 1)
        return jnp.where(low == row_low, 1.0, 0.0).astype(bf16)

    def add_row(sums, slots, fields, right, y):
        mask = lax.shift_right_logical(spread(slots, y, HIGH), 4) == row_high
        left = jnp.concatenate([jnp.where(mask, spread(field, y, HIGH), 0.0) for field in fields], axis=0)
        return sums + lax.dot_general(
            left.astype(bf16), right, (((1,), (1,)), ((), ())), preferred_element_type=f32
        )

    def split(high, low, weighted):
        upper = weighted.astype(bf16).astype(f32)
        high[...] = upper
        low[...] = weighted - upper

    for x in range(nx):
        here = cond[x]
        if x > 0:
            lx[x] = harmonic(cond[x - 1], here)
        right = jnp.where(lane == nz - 1, 0.0, harmonic(here, pltpu.roll(here, nz - 1, 1)))
        up = jnp.where(row == ny - 1, 0.0, harmonic(here, pltpu.roll(here, ny - 1, 0)))
        lz[x] = right
        lzleft[x] = pltpu.roll(right, 1, 1)
        ly[x] = up
        lydown[x] = pltpu.roll(up, 1, 0)
    for x in range(nx):
        phase = m[x]
        cap = jnp.where(phase == 0, 1.0, jnp.where(phase == 1, 2.0, 1.5)).astype(f32)
        whole = cap + lz[x] + lzleft[x] + ly[x] + lydown[x]
        if x > 0:
            whole = whole + lx[x]
        if x < nx - 1:
            whole = whole + lx[x + 1]
        diag[x] = whole

    def apply(field, x):
        v = field[x]
        out = diag[x] * v
        if x > 0:
            out = out - lx[x] * field[x - 1]
        if x < nx - 1:
            out = out - lx[x + 1] * field[x + 1]
        out = out - ly[x] * pltpu.roll(v, ny - 1, 0) - lydown[x] * pltpu.roll(v, 1, 0)
        return out - lz[x] * pltpu.roll(v, nz - 1, 1) - lzleft[x] * pltpu.roll(v, 1, 1)

    for x in range(nx):
        z1[x] = apply(r, x)

    def begin_sketch(x, sums):
        split(parts.at[0, x], parts.at[1, x], d[x] * r[x])
        for y in range(ny):
            right = low_rows(slot.at[x], y)
            onehot[x, y] = right
            sums = add_row(sums, slot.at[x], (parts.at[0, x], parts.at[1, x]), right, y)
        return sums

    sums = lax.fori_loop(0, nx, begin_sketch, jnp.zeros((2 * HIGH, LOW), f32))
    mine[...] = jnp.zeros((HIGH, SKETCH), f32)
    mine[:, 0:LOW] = sums[:HIGH] + sums[HIGH:]
    for turn in range(2, ngy):
        hear(turn - 1)
        tell(turn)

    arrive(0, hx_first, hy_first)
    for s in (0, 1):
        e = edge_x[s]
        link = harmonic(hx_first[s, 0], cond[e])
        lx[nx * s] = link
        z1[e] = z1[e] + link * (r[e] - hx_first[s, 1])
    for s in (0, 1):
        for x in range(nx):
            here, there = pl.ds(x, 1), pl.ds(nx + x, 1)
            link = harmonic(hy_first[s, there, :], py_first[s, there, :])
            lyb[s, here, :] = link
            flux = link * (py_first[s, here, :] - hy_first[s, here, :])
            after = z1[x, pl.ds(edge_y[s], 1), :] + flux
            z1[x, pl.ds(edge_y[s], 1), :] = after
            py_z[s, here, :] = after
    begin(2, lambda s: z1.at[edge_x[s]], hx_z, lambda s: py_z.at[s], hy_z)
    for x in range(nx):
        out = apply(z1, x)
        for s in (0, 1):
            if x == edge_x[s]:
                out = out + lx[nx * s] * z1[x]
        z2[x] = out
        for s in (0, 1):
            at = (x, pl.ds(edge_y[s], 1), slice(None))
            z2[at] = z2[at] + lyb[s, pl.ds(x, 1), :] * py_z[s, pl.ds(x, 1), :]
    sums = jnp.zeros((4 * HIGH, LOW), f32)
    for x in range(nx):
        split(parts.at[0, x], parts.at[1, x], d[x] * z1[x])
        split(parts.at[2, x], parts.at[3, x], d[x] * z2[x])
        for y in range(ny):
            sums = add_row(sums, slot.at[x], [parts.at[k, x] for k in range(4)], onehot[x, y], y)
    arrive(1, hx_early, hy_early)
    edge_sums = jnp.zeros((2 * HIGH, LOW), f32)
    for s in (0, 1):
        split(wedge.at[0, s], wedge.at[1, s], -lx[nx * s] * z1[edge_x[s]] * hx_early[s, 1])
        sedge[s] = hx_early[s, 0].astype(jnp.int32)
        for x in range(nx):
            at = pl.ds(s * nx + x, 1)
            edge = -lyb[s, pl.ds(x, 1), :] * py_z[s, pl.ds(x, 1), :] * hy_early[s, pl.ds(nx + x, 1), :]
            upper = edge.astype(bf16).astype(f32)
            wedge[0, 2, at, :] = upper
            wedge[1, 2, at, :] = edge - upper
            sedge[2, at, :] = hy_early[s, pl.ds(x, 1), :].astype(jnp.int32)
    for t in range(3):
        for y in range(ny if t < 2 else 2 * nx):
            edge_sums = add_row(edge_sums, sedge.at[t], (wedge.at[0, t], wedge.at[1, t]), low_rows(sedge.at[t], y), y)
    mine[:, LOW : 2 * LOW] = sums[:HIGH] + sums[HIGH : 2 * HIGH]
    mine[:, 2 * LOW : 3 * LOW] = (
        sums[2 * HIGH : 3 * HIGH] + sums[3 * HIGH :] + edge_sums[:HIGH] + edge_sums[HIGH:]
    )

    def share(step, carry):
        pltpu.make_async_remote_copy(
            src_ref=mine,
            dst_ref=gathered.at[me],
            send_sem=share_sem.at[0],
            recv_sem=share_sem.at[1],
            device_id=peer(step),
            device_id_type=MESH,
        ).start()
        return carry

    if ngy > 1:
        hear(ngy - 1)
    lax.fori_loop(1, count, share, 0)
    gathered[me] = mine[...]
    arrive(2, hx_z, hy_z)
    for s in (0, 1):
        z2[edge_x[s]] = z2[edge_x[s]] - lx[nx * s] * hx_z[s]
        for x in range(nx):
            at = (x, pl.ds(edge_y[s], 1), slice(None))
            z2[at] = z2[at] - lyb[s, pl.ds(x, 1), :] * hy_z[s, pl.ds(x, 1), :]
    others = gathered.at[pl.ds(0, count - 1)]
    shared = pltpu.make_async_remote_copy(
        src_ref=others,
        dst_ref=others,
        send_sem=share_sem.at[0],
        recv_sem=share_sem.at[1],
        device_id=peer(1),
        device_id_type=MESH,
    )
    shared.wait_recv()
    summed = jnp.sum(gathered[...], axis=0)
    c0, c1 = coefficients(*(summed[:, k * LOW : (k + 1) * LOW] for k in range(3)))
    for x in range(nx):
        answer[x] = c0 * r[x] + c1 * z1[x]
        rest[x] = r[x] - c0 * z1[x] - c1 * z2[x]
    shared.wait_send()
    settle(0, has_x, sent.at[0], bulk_x, "wait_send")
    settle(1, has_y, sent.at[1], bulk_y, "wait_send")


def put_out(answer, rest, answer_out, rest_out, sem):
    one = pltpu.make_async_copy(answer, answer_out, sem.at[0])
    two = pltpu.make_async_copy(rest, rest_out, sem.at[1])
    one.start()
    two.start()
    one.wait()
    two.wait()


def body(ngx, ngy, f, w, m, s, d):
    nx, ny, nz = f.shape
    count = ngx * ngy
    vm = lambda shape, dtype=f32: pltpu.VMEM(shape, dtype)
    block = (nx, ny, nz)
    assert 2 * nx <= ny
    answer, rest = pl.pallas_call(
        functools.partial(kernel, ngx, ngy, nx, ny, nz),
        out_shape=(vm(block), vm(block)),
        in_specs=[pl.BlockSpec(memory_space=pl.ANY)] * 5,
        out_specs=[pl.BlockSpec(memory_space=pltpu.VMEM)] * 2,
        scratch_shapes=[
            vm(block), vm(block),
            vm(block), vm(block), vm(block, jnp.int32), vm(block, jnp.int32), vm(block),
            vm(block), vm(block),
            vm((nx + 1, ny, nz)), vm(block), vm(block), vm(block), vm(block), vm((2, nx, nz)),
            vm((nx, ny, LOW, nz), bf16), vm((4, nx, ny, nz)), vm((2, 3, ny, nz)), vm((3, ny, nz), jnp.int32),
            vm((2, 2, ny, nz)), vm((2, 2, ny, nz)), vm((2, ny, nz)), vm((2, 2 * nx, nz)), vm((2, 2 * nx, nz)), vm((2, nx, nz)),
            vm((2, 2, ny, nz)), vm((2, 2, ny, nz)), vm((2, 2 * nx, nz)), vm((2, 2 * nx, nz)), vm((2, nx, nz)),
            vm((2, 5, ny, nz)), vm((2, 5, nx, nz)),
            vm((HIGH, SKETCH)), vm((count, HIGH, SKETCH)),
            pltpu.SemaphoreType.DMA((5,)),
            pltpu.SemaphoreType.DMA((2,)),
            pltpu.SemaphoreType.DMA((2, 3)),
            pltpu.SemaphoreType.DMA((2,)),
            pltpu.SemaphoreType.REGULAR((max(ngy - 1, 1),)),
        ],
        compiler_params=pltpu.CompilerParams(collective_id=0, has_side_effects=True),
        name="sketched_gmres",
    )(f, w, m, s, d)
    return pl.pallas_call(
        put_out,
        out_shape=(jax.ShapeDtypeStruct(block, f32), jax.ShapeDtypeStruct(block, f32)),
        in_specs=[pl.BlockSpec(memory_space=pltpu.VMEM)] * 2,
        out_specs=[pl.BlockSpec(memory_space=pl.ANY)] * 2,
        scratch_shapes=[pltpu.SemaphoreType.DMA((2,))],
        name="put_out",
    )(pltpu.with_memory_space_constraint(answer, pltpu.VMEM), pltpu.with_memory_space_constraint(rest, pltpu.VMEM))


def solution(mesh):
    spec = P(("parts", "gx"), "gy", None)
    return jax.shard_map(
        functools.partial(body, mesh.shape["gx"], mesh.shape["gy"]),
        mesh=mesh,
        in_specs=(spec,) * 5,
        out_specs=(spec, spec),
        check_vma=False,
    )
```

```python
import functools

import jax
import jax.numpy as jnp
from jax import lax
from jax.experimental import pallas as pl
from jax.experimental.pallas import tpu as pltpu
from jax.sharding import PartitionSpec as P

SKETCH = 128
LOW = 16
HIGH = SKETCH // LOW
MESH = pl.DeviceIdType.MESH
epsilon = 1e-06
highest = lax.Precision.HIGHEST
f32 = jnp.float32
bf16 = jnp.bfloat16


def harmonic(first, second):
    return 2.0 * first * second / (first + second)


def total(field):
    return jnp.sum(jnp.sum(field, axis=1, keepdims=True), axis=0, keepdims=True)


def coefficients(s0, s1, s2):
    inv_beta2 = 1.0 / (total(s0 * s0) + epsilon)
    h00 = total(s0 * s1) * inv_beta2
    t0 = s1 - h00 * s0
    w1 = s2 - h00 * s1
    n0sq = total(t0 * t0) * inv_beta2 + epsilon
    cross = total(s0 * w1) * inv_beta2
    along = total(t0 * w1) * inv_beta2
    whole = total(w1 * w1) * inv_beta2
    inv_n0sq = 1.0 / n0sq
    h11 = along * inv_n0sq
    shift = epsilon * inv_beta2
    left = whole - cross * cross * (1.0 + shift) - h11 * h11 * (n0sq + epsilon) + 2.0 * cross * h11 * h00 * shift
    n1sq = jnp.maximum(left, 0.0) * inv_n0sq + epsilon
    minor = h00 * h11 - cross
    inv_det = 1.0 / (minor * minor + n1sq * (h00 * h00 + n0sq))
    return (minor * (h11 + h00) + h00 * n1sq) * inv_det, -minor * inv_det


def kernel(
    ngx, ngy, nx, ny, nz,
    f_hbm, w_hbm, m_hbm, s_hbm, d_hbm,
    answer, rest,
    z1, z2, r, w, m, slot, d, cond, diag, lx, ly, lydown, lz, lzleft, lyb, onehot, onehot_edge, parts, wedge, sedge,
    hx_first, hx_early, hx_z, hy_first, hy_early, hy_z,
    px_first, px_early, py_first, py_early, py_z,
    bulk_x, bulk_y, mine, gathered, load_sem, sent, landed, share_sem, known,
):
    gx = lax.axis_index("gx")
    gy = lax.axis_index("gy")
    count = ngx * ngy
    me = gx * ngy + gy


    def peer(step):
        other = lax.rem(me + step, count)
        return {"gx": lax.div(other, ngy), "gy": lax.rem(other, ngy)}

    barrier = pltpu.get_barrier_semaphore()

    for step in range(1, ngx):
        other = {"gx": lax.rem(gx + step, ngx), "gy": gy}
        pl.semaphore_signal(barrier, inc=1, device_id=other, device_id_type=MESH)

    has_x = (gx > 0, gx < ngx - 1)
    has_y = (gy > 0, gy < ngy - 1)
    to_x = ({"gx": gx - 1, "gy": gy}, {"gx": gx + 1, "gy": gy})
    to_y = ({"gx": gx, "gy": gy - 1}, {"gx": gx, "gy": gy + 1})
    for s in (0, 1):

        @pl.when(has_y[s])
        def _():
            pl.semaphore_signal(barrier, inc=1, device_id=to_y[s], device_id_type=MESH)

    loads = [
        pltpu.make_async_copy(src, dst, load_sem.at[i])
        for i, (src, dst) in enumerate(
            ((w_hbm, w), (m_hbm, m), (f_hbm, r), (s_hbm, slot), (d_hbm, d))
        )
    ]
    for load in loads:
        load.start()

    n_y = has_y[0].astype(jnp.int32) + has_y[1].astype(jnp.int32)

    def tell(side):
        pl.semaphore_signal(known.at[side], inc=1, device_id=to_y[side], device_id_type=MESH)

    def pass_on(side):
        pl.semaphore_wait(known.at[side], 1)
        tell(side)

    middle = jnp.logical_and(has_y[0], has_y[1])

    edge_x = (0, nx - 1)
    edge_y = (0, ny - 1)

    def remote(src, dst, axis, index, side, target):
        return pltpu.make_async_remote_copy(
            src_ref=src,
            dst_ref=dst.at[1 - side],
            send_sem=sent.at[axis],
            recv_sem=landed.at[axis, index],
            device_id=target,
            device_id_type=MESH,
        )

    def begin(index, src_x, dst_x, src_y, dst_y):
        for s in (0, 1):
            pl.when(has_x[s])(remote(src_x(s), dst_x, 0, index, s, to_x[s]).start)
        for s in (0, 1):
            pl.when(has_y[s])(remote(src_y(s), dst_y, 1, index, s, to_y[s]).start)

    def settle(axis, has, sem, ref, kind):
        target = to_x[0] if axis == 0 else to_y[0]

        def wait(part):
            copy = pltpu.make_async_remote_copy(
                src_ref=part, dst_ref=part, send_sem=sem, recv_sem=sem, device_id=target, device_id_type=MESH
            )
            return getattr(copy, kind)

        pl.when(jnp.logical_and(has[0], has[1]))(wait(ref))
        pl.when(jnp.logical_xor(has[0], has[1]))(wait(ref.at[0]))

    def arrive(index, dst_x, dst_y):
        settle(0, has_x, landed.at[0, index], dst_x, "wait_recv")
        settle(1, has_y, landed.at[1, index], dst_y, "wait_recv")

    loads[0].wait()
    loads[1].wait()
    for x in range(nx):
        phase = m[x]
        cond[x] = jnp.where(phase == 0, 0.2, jnp.where(phase == 1, 1.0, 0.6)).astype(f32) * (0.5 + w[x])
    loads[2].wait()
    for s in (0, 1):
        e = edge_x[s]
        px_first[s, 0] = cond[e]
        px_first[s, 1] = r[e]
        for x in range(nx):
            py_first[s, pl.ds(x, 1), :] = r[x, pl.ds(edge_y[s], 1), :]
            py_first[s, pl.ds(nx + x, 1), :] = cond[x, pl.ds(edge_y[s], 1), :]

        @pl.when(jnp.logical_not(has_x[s]))
        def _():
            hx_first[s] = jnp.zeros((2, ny, nz), f32)
            hx_early[s] = jnp.zeros((2, ny, nz), f32)
            hx_z[s] = jnp.zeros((ny, nz), f32)

        @pl.when(jnp.logical_not(has_y[s]))
        def _():
            hy_first[s] = jnp.zeros((2 * nx, nz), f32)
            hy_early[s] = jnp.zeros((2 * nx, nz), f32)
            hy_z[s] = jnp.zeros((nx, nz), f32)

    pl.semaphore_wait(barrier, ngx - 1 + n_y)
    begin(0, lambda s: px_first.at[s], hx_first, lambda s: py_first.at[s], hy_first)
    if ngy > 1:
        pl.when(gy == 0)(functools.partial(tell, 1))
        pl.when(gy == ngy - 1)(functools.partial(tell, 0))
        pl.when(middle)(functools.partial(pass_on, 1))
    loads[3].wait()
    loads[4].wait()
    for s in (0, 1):
        e = edge_x[s]
        px_early[s, 0] = slot[e].astype(f32)
        px_early[s, 1] = d[e]
        for x in range(nx):
            py_early[s, pl.ds(x, 1), :] = slot[x, pl.ds(edge_y[s], 1), :].astype(f32)
            py_early[s, pl.ds(nx + x, 1), :] = d[x, pl.ds(edge_y[s], 1), :]
    begin(1, lambda s: px_early.at[s], hx_early, lambda s: py_early.at[s], hy_early)

    lane = lax.broadcasted_iota(jnp.int32, (ny, nz), 1)
    row = lax.broadcasted_iota(jnp.int32, (ny, nz), 0)
    row_high = lax.broadcasted_iota(jnp.int32, (HIGH, nz), 0)
    row_low = lax.broadcasted_iota(jnp.int32, (LOW, nz), 0)

    def spread(ref, y, rows):
        part = ref[pl.ds(y, 8, stride=0), :]
        return part if rows == 8 else jnp.concatenate([part] * (rows // 8), axis=0)

    def low_rows(slots, y):
        low = jnp.bitwise_and(spread(slots, y, LOW), LOW - 1)
        return jnp.where(low == row_low, 1.0, 0.0).astype(bf16)

    def add_row(sums, slots, fields, right, y):
        mask = lax.shift_right_logical(spread(slots, y, HIGH), 4) == row_high
        left = jnp.concatenate([jnp.where(mask, spread(field, y, HIGH), 0.0) for field in fields], axis=0)
        return sums + lax.dot_general(
            left.astype(bf16), right, (((1,), (1,)), ((), ())), preferred_element_type=f32
        )

    def split(high, low, weighted):
        upper = weighted.astype(bf16).astype(f32)
        high[...] = upper
        low[...] = weighted - upper

    for x in range(nx):
        here = cond[x]
        if x > 0:
            lx[x] = harmonic(cond[x - 1], here)
        right = jnp.where(lane == nz - 1, 0.0, harmonic(here, pltpu.roll(here, nz - 1, 1)))
        up = jnp.where(row == ny - 1, 0.0, harmonic(here, pltpu.roll(here, ny - 1, 0)))
        lz[x] = right
        lzleft[x] = pltpu.roll(right, 1, 1)
        ly[x] = up
        lydown[x] = pltpu.roll(up, 1, 0)
    for x in range(nx):
        phase = m[x]
        cap = jnp.where(phase == 0, 1.0, jnp.where(phase == 1, 2.0, 1.5)).astype(f32)
        whole = cap + lz[x] + lzleft[x] + ly[x] + lydown[x]
        if x > 0:
            whole = whole + lx[x]
        if x < nx - 1:
            whole = whole + lx[x + 1]
        diag[x] = whole

    def apply(field, x):
        v = field[x]
        out = diag[x] * v
        if x > 0:
            out = out - lx[x] * field[x - 1]
        if x < nx - 1:
            out = out - lx[x + 1] * field[x + 1]
        out = out - ly[x] * pltpu.roll(v, ny - 1, 0) - lydown[x] * pltpu.roll(v, 1, 0)
        return out - lz[x] * pltpu.roll(v, nz - 1, 1) - lzleft[x] * pltpu.roll(v, 1, 1)

    for x in range(nx):
        z1[x] = apply(r, x)

    def begin_sketch(x, sums):
        split(parts.at[0, x], parts.at[1, x], d[x] * r[x])
        for y in range(ny):
            right = low_rows(slot.at[x], y)
            onehot[x, y] = right
            sums = add_row(sums, slot.at[x], (parts.at[0, x], parts.at[1, x]), right, y)
        return sums

    sums = lax.fori_loop(0, nx, begin_sketch, jnp.zeros((2 * HIGH, LOW), f32))
    mine[...] = jnp.zeros((HIGH, SKETCH), f32)
    mine[:, 0:LOW] = sums[:HIGH] + sums[HIGH:]
    if ngy > 1:
        pl.when(middle)(functools.partial(pass_on, 0))

    arrive(0, hx_first, hy_first)
    for s in (0, 1):
        e = edge_x[s]
        link = harmonic(hx_first[s, 0], cond[e])
        lx[nx * s] = link
        z1[e] = z1[e] + link * (r[e] - hx_first[s, 1])
    for s in (0, 1):
        for x in range(nx):
            here, there = pl.ds(x, 1), pl.ds(nx + x, 1)
            link = harmonic(hy_first[s, there, :], py_first[s, there, :])
            lyb[s, here, :] = link
            flux = link * (py_first[s, here, :] - hy_first[s, here, :])
            after = z1[x, pl.ds(edge_y[s], 1), :] + flux
            z1[x, pl.ds(edge_y[s], 1), :] = after
            py_z[s, here, :] = after
    begin(2, lambda s: z1.at[edge_x[s]], hx_z, lambda s: py_z.at[s], hy_z)
    chains = [jnp.zeros((4 * HIGH, LOW), f32) for _ in range(2)]
    for x in range(nx):
        out = apply(z1, x)
        for s in (0, 1):
            if x == edge_x[s]:
                out = out + lx[nx * s] * z1[x]
        z2[x] = out
        for s in (0, 1):
            at = (x, pl.ds(edge_y[s], 1), slice(None))
            z2[at] = z2[at] + lyb[s, pl.ds(x, 1), :] * py_z[s, pl.ds(x, 1), :]
        split(parts.at[0, x], parts.at[1, x], d[x] * z1[x])
        split(parts.at[2, x], parts.at[3, x], d[x] * z2[x])
        for y in range(ny):
            chains[y % 2] = add_row(chains[y % 2], slot.at[x], [parts.at[k, x] for k in range(4)], onehot[x, y], y)
    arrive(1, hx_early, hy_early)
    edge_chains = [jnp.zeros((2 * HIGH, LOW), f32) for _ in range(2)]
    for s in (0, 1):
        split(wedge.at[0, s], wedge.at[1, s], -lx[nx * s] * z1[edge_x[s]] * hx_early[s, 1])
        sedge[s] = hx_early[s, 0].astype(jnp.int32)
        for x in range(nx):
            at = pl.ds(s * nx + x, 1)
            edge = -lyb[s, pl.ds(x, 1), :] * py_z[s, pl.ds(x, 1), :] * hy_early[s, pl.ds(nx + x, 1), :]
            upper = edge.astype(bf16).astype(f32)
            wedge[0, 2, at, :] = upper
            wedge[1, 2, at, :] = edge - upper
            sedge[2, at, :] = hy_early[s, pl.ds(x, 1), :].astype(jnp.int32)
    for t in range(3):
        for y in range(ny if t < 2 else 2 * nx):
            onehot_edge[t, y] = low_rows(sedge.at[t], y)
    for t in range(3):
        for y in range(ny if t < 2 else 2 * nx):
            edge_chains[y % 2] = add_row(edge_chains[y % 2], sedge.at[t], (wedge.at[0, t], wedge.at[1, t]), onehot_edge[t, y], y)
    def placed(block, k):
        wide = jnp.concatenate([block, jnp.zeros((HIGH, SKETCH - LOW), f32)], axis=1)
        return pltpu.roll(wide, k * LOW, 1)

    out = mine[...]
    for sums, edge_sums in zip(chains, edge_chains):
        out = out + placed(sums[:HIGH] + sums[HIGH : 2 * HIGH], 1)
        out = out + placed(sums[2 * HIGH : 3 * HIGH] + sums[3 * HIGH :], 2)
        out = out + placed(edge_sums[:HIGH] + edge_sums[HIGH:], 2)
    mine[...] = out

    def share(step, carry):
        pltpu.make_async_remote_copy(
            src_ref=mine,
            dst_ref=gathered.at[me],
            send_sem=share_sem.at[0],
            recv_sem=share_sem.at[1],
            device_id=peer(step),
            device_id_type=MESH,
        ).start()
        return carry

    for s in (0, 1):

        @pl.when(jnp.logical_and(has_y[1 - s], jnp.logical_not(has_y[s])))
        def _():
            pl.semaphore_wait(known.at[s], 1)

    lax.fori_loop(1, count, share, 0)
    gathered[me] = mine[...]
    arrive(2, hx_z, hy_z)
    for s in (0, 1):
        z2[edge_x[s]] = z2[edge_x[s]] - lx[nx * s] * hx_z[s]
        for x in range(nx):
            at = (x, pl.ds(edge_y[s], 1), slice(None))
            z2[at] = z2[at] - lyb[s, pl.ds(x, 1), :] * hy_z[s, pl.ds(x, 1), :]
    others = gathered.at[pl.ds(0, count - 1)]
    shared = pltpu.make_async_remote_copy(
        src_ref=others,
        dst_ref=others,
        send_sem=share_sem.at[0],
        recv_sem=share_sem.at[1],
        device_id=peer(1),
        device_id_type=MESH,
    )
    shared.wait_recv()
    summed = jnp.sum(gathered[...], axis=0)
    first_lanes = lax.broadcasted_iota(jnp.int32, (HIGH, SKETCH), 1) < LOW
    c0, c1 = coefficients(
        *(jnp.where(first_lanes, pltpu.roll(summed, SKETCH - k * LOW, 1) if k else summed, 0.0) for k in range(3))
    )
    for x in range(nx):
        answer[x] = c0 * r[x] + c1 * z1[x]
        rest[x] = r[x] - c0 * z1[x] - c1 * z2[x]
    shared.wait_send()
    settle(0, has_x, sent.at[0], bulk_x, "wait_send")
    settle(1, has_y, sent.at[1], bulk_y, "wait_send")


def put_out(answer, rest, answer_out, rest_out, sem):
    one = pltpu.make_async_copy(answer, answer_out, sem.at[0])
    two = pltpu.make_async_copy(rest, rest_out, sem.at[1])
    one.start()
    two.start()
    one.wait()
    two.wait()


def body(ngx, ngy, f, w, m, s, d):
    nx, ny, nz = f.shape
    count = ngx * ngy
    vm = lambda shape, dtype=f32: pltpu.VMEM(shape, dtype)
    block = (nx, ny, nz)
    assert 2 * nx <= ny
    answer, rest = pl.pallas_call(
        functools.partial(kernel, ngx, ngy, nx, ny, nz),
        out_shape=(vm(block), vm(block)),
        in_specs=[pl.BlockSpec(memory_space=pl.ANY)] * 5,
        out_specs=[pl.BlockSpec(memory_space=pltpu.VMEM)] * 2,
        scratch_shapes=[
            vm(block), vm(block),
            vm(block), vm(block), vm(block, jnp.int32), vm(block, jnp.int32), vm(block),
            vm(block), vm(block),
            vm((nx + 1, ny, nz)), vm(block), vm(block), vm(block), vm(block), vm((2, nx, nz)),
            vm((nx, ny, LOW, nz), bf16), vm((3, ny, LOW, nz), bf16), vm((4, nx, ny, nz)), vm((2, 3, ny, nz)), vm((3, ny, nz), jnp.int32),
            vm((2, 2, ny, nz)), vm((2, 2, ny, nz)), vm((2, ny, nz)), vm((2, 2 * nx, nz)), vm((2, 2 * nx, nz)), vm((2, nx, nz)),
            vm((2, 2, ny, nz)), vm((2, 2, ny, nz)), vm((2, 2 * nx, nz)), vm((2, 2 * nx, nz)), vm((2, nx, nz)),
            vm((2, 5, ny, nz)), vm((2, 5, nx, nz)),
            vm((HIGH, SKETCH)), vm((count, HIGH, SKETCH)),
            pltpu.SemaphoreType.DMA((5,)),
            pltpu.SemaphoreType.DMA((2,)),
            pltpu.SemaphoreType.DMA((2, 3)),
            pltpu.SemaphoreType.DMA((2,)),
            pltpu.SemaphoreType.REGULAR((2,)),
        ],
        compiler_params=pltpu.CompilerParams(collective_id=0, has_side_effects=True),
        name="sketched_gmres",
    )(f, w, m, s, d)
    return pl.pallas_call(
        put_out,
        out_shape=(jax.ShapeDtypeStruct(block, f32), jax.ShapeDtypeStruct(block, f32)),
        in_specs=[pl.BlockSpec(memory_space=pltpu.VMEM)] * 2,
        out_specs=[pl.BlockSpec(memory_space=pl.ANY)] * 2,
        scratch_shapes=[pltpu.SemaphoreType.DMA((2,))],
        name="put_out",
    )(pltpu.with_memory_space_constraint(answer, pltpu.VMEM), pltpu.with_memory_space_constraint(rest, pltpu.VMEM))


def solution(mesh):
    spec = P(("parts", "gx"), "gy", None)
    return jax.shard_map(
        functools.partial(body, mesh.shape["gx"], mesh.shape["gy"]),
        mesh=mesh,
        in_specs=(spec,) * 5,
        out_specs=(spec, spec),
        check_vma=False,
    )
```

```python
import functools

import jax
import jax.numpy as jnp
from jax import lax
from jax.experimental import pallas as pl
from jax.experimental.pallas import tpu as pltpu
from jax.sharding import PartitionSpec as P

SKETCH = 128
LOW = 16
HIGH = SKETCH // LOW
WIDE = 32
MESH = pl.DeviceIdType.MESH
epsilon = 1e-06
highest = lax.Precision.HIGHEST
f32 = jnp.float32
bf16 = jnp.bfloat16


def harmonic(first, second):
    return 2.0 * first * second / (first + second)


def total(field):
    return jnp.sum(jnp.sum(field, axis=1, keepdims=True), axis=0, keepdims=True)


def coefficients(s0, s1, s2):
    inv_beta2 = 1.0 / (total(s0 * s0) + epsilon)
    h00 = total(s0 * s1) * inv_beta2
    t0 = s1 - h00 * s0
    w1 = s2 - h00 * s1
    n0sq = total(t0 * t0) * inv_beta2 + epsilon
    cross = total(s0 * w1) * inv_beta2
    along = total(t0 * w1) * inv_beta2
    whole = total(w1 * w1) * inv_beta2
    inv_n0sq = 1.0 / n0sq
    h11 = along * inv_n0sq
    shift = epsilon * inv_beta2
    left = whole - cross * cross * (1.0 + shift) - h11 * h11 * (n0sq + epsilon) + 2.0 * cross * h11 * h00 * shift
    n1sq = jnp.maximum(left, 0.0) * inv_n0sq + epsilon
    minor = h00 * h11 - cross
    inv_det = 1.0 / (minor * minor + n1sq * (h00 * h00 + n0sq))
    return (minor * (h11 + h00) + h00 * n1sq) * inv_det, -minor * inv_det


def kernel(
    ngx, ngy, nx, ny, nz,
    f_hbm, w_hbm, m_hbm, s_hbm, d_hbm,
    answer, rest,
    z1, z2, r, w, m, slot, d, cond, diag, lx, ly, lydown, lz, lzleft, lyb, onehot, highs, onehot_edge, parts, wedge, sedge,
    hx_first, hx_early, hx_z, hy_first, hy_early, hy_z,
    px_first, px_early, py_first, py_early, py_z,
    bulk_x, bulk_y, mine, gathered, load_sem, sent, landed, beside, share_sem, known,
):
    gx = lax.axis_index("gx")
    gy = lax.axis_index("gy")
    count = ngx * ngy
    me = gx * ngy + gy


    mine_at = gy * ngx + gx

    def peer(step):
        other = step + (step >= mine_at).astype(jnp.int32)
        return {"gx": lax.rem(other, ngx), "gy": lax.div(other, ngx)}

    barrier = pltpu.get_barrier_semaphore()

    has_x = (gx > 0, gx < ngx - 1)
    has_y = (gy > 0, gy < ngy - 1)
    to_x = ({"gx": gx - 1, "gy": gy}, {"gx": gx + 1, "gy": gy})
    to_y = ({"gx": gx, "gy": gy - 1}, {"gx": gx, "gy": gy + 1})
    for s in (0, 1):

        @pl.when(has_y[s])
        def _():
            pl.semaphore_signal(barrier, inc=1, device_id=to_y[s], device_id_type=MESH)

    for step in range(1, ngx):
        other = {"gx": lax.rem(gx + step, ngx), "gy": gy}
        pl.semaphore_signal(barrier, inc=1, device_id=other, device_id_type=MESH)

    loads = [
        pltpu.make_async_copy(src, dst, load_sem.at[i])
        for i, src, dst in ((0, w_hbm, w), (0, m_hbm, m), (1, f_hbm, r), (2, s_hbm, slot), (2, d_hbm, d))
    ]
    for load in loads:
        load.start()

    n_y = has_y[0].astype(jnp.int32) + has_y[1].astype(jnp.int32)

    def tell(side):
        pl.semaphore_signal(known.at[side], inc=1, device_id=to_y[side], device_id_type=MESH)

    def pass_on(side):
        pl.semaphore_wait(known.at[side], 1)
        tell(side)

    middle = jnp.logical_and(has_y[0], has_y[1])

    edge_x = (0, nx - 1)
    edge_y = (0, ny - 1)

    def arrival(axis, index, side):
        if axis == 0 and index == 1:
            return beside.at[side]
        return landed.at[(0, None, 1)[index] if axis == 0 else 2 + index]

    def remote(src, dst, axis, index, side, target):
        return pltpu.make_async_remote_copy(
            src_ref=src,
            dst_ref=dst.at[1 - side],
            send_sem=sent.at[axis],
            recv_sem=arrival(axis, index, 1 - side),
            device_id=target,
            device_id_type=MESH,
        )

    def begin(index, src_x, dst_x, src_y, dst_y):
        for s in (0, 1):
            pl.when(has_y[s])(remote(src_y(s), dst_y, 1, index, s, to_y[s]).start)
        for s in (0, 1):
            pl.when(has_x[s])(remote(src_x(s), dst_x, 0, index, s, to_x[s]).start)

    def settle(axis, has, sem, ref, kind):
        target = to_x[0] if axis == 0 else to_y[0]

        def wait(part):
            copy = pltpu.make_async_remote_copy(
                src_ref=part, dst_ref=part, send_sem=sem, recv_sem=sem, device_id=target, device_id_type=MESH
            )
            return getattr(copy, kind)

        pl.when(jnp.logical_and(has[0], has[1]))(wait(ref))
        pl.when(jnp.logical_xor(has[0], has[1]))(wait(ref.at[0]))

    def arrive(index, dst_x, dst_y):
        settle(0, has_x, arrival(0, index, 0), dst_x, "wait_recv")
        settle(1, has_y, arrival(1, index, 0), dst_y, "wait_recv")

    far = jnp.bitwise_and(gx, 1)
    near = 1 - far

    def arrive_beside(side):
        copy = pltpu.make_async_remote_copy(
            src_ref=hx_early.at[side],
            dst_ref=hx_early.at[side],
            send_sem=sent.at[0],
            recv_sem=beside.at[side],
            device_id=to_x[0],
            device_id_type=MESH,
        )
        pl.when(jnp.logical_or(jnp.logical_and(side == 0, has_x[0]), jnp.logical_and(side == 1, has_x[1])))(copy.wait_recv)

    two_blocks = parts.at[pl.ds(0, nx // 2)]

    def both_loaded(i):
        pltpu.make_async_copy(two_blocks, two_blocks, load_sem.at[i]).wait()

    both_loaded(0)
    for x in range(nx):
        phase = m[x]
        cond[x] = jnp.where(phase == 0, 0.2, jnp.where(phase == 1, 1.0, 0.6)).astype(f32) * (0.5 + w[x])
    loads[2].wait()
    for s in (0, 1):
        e = edge_x[s]
        px_first[s, 0] = cond[e]
        px_first[s, 1] = r[e]
        for x in range(nx):
            py_first[s, pl.ds(x, 1), :] = r[x, pl.ds(edge_y[s], 1), :]
            py_first[s, pl.ds(nx + x, 1), :] = cond[x, pl.ds(edge_y[s], 1), :]

        @pl.when(jnp.logical_not(has_x[s]))
        def _():
            hx_first[s] = jnp.zeros((2, ny, nz), f32)
            hx_early[s] = jnp.zeros((2, ny, nz), f32)
            hx_z[s] = jnp.zeros((ny, nz), f32)

        @pl.when(jnp.logical_not(has_y[s]))
        def _():
            hy_first[s] = jnp.zeros((2 * nx, nz), f32)
            hy_early[s] = jnp.zeros((2 * nx, nz), f32)
            hy_z[s] = jnp.zeros((nx, nz), f32)

    pl.semaphore_wait(barrier, ngx - 1 + n_y)
    begin(0, lambda s: px_first.at[s], hx_first, lambda s: py_first.at[s], hy_first)
    if ngy > 1:
        pl.when(gy == 0)(functools.partial(tell, 1))
        pl.when(gy == ngy - 1)(functools.partial(tell, 0))
    both_loaded(2)
    for s in (0, 1):
        e = edge_x[s]
        px_early[s, 0] = slot[e].astype(f32)
        px_early[s, 1] = d[e]
        for x in range(nx):
            py_early[s, pl.ds(x, 1), :] = slot[x, pl.ds(edge_y[s], 1), :].astype(f32)
            py_early[s, pl.ds(nx + x, 1), :] = d[x, pl.ds(edge_y[s], 1), :]
    begin(1, lambda s: px_early.at[s], hx_early, lambda s: py_early.at[s], hy_early)

    lane = lax.broadcasted_iota(jnp.int32, (ny, nz), 1)
    row = lax.broadcasted_iota(jnp.int32, (ny, nz), 0)
    place = lax.broadcasted_iota(jnp.int32, (HIGH, nz), 0)
    row_half = lax.shift_right_logical(place, 2)
    row_high = 2 * row_half + 4 * jnp.bitwise_and(lax.shift_right_logical(place, 1), 1) + jnp.bitwise_and(place, 1)
    row_low = lax.broadcasted_iota(jnp.int32, (LOW, nz), 0)
    row_wide = lax.broadcasted_iota(jnp.int32, (WIDE, nz), 0)

    def spread(ref, y, rows):
        part = ref[pl.ds(y, 8, stride=0), :]
        return part if rows == 8 else jnp.concatenate([part] * (rows // 8), axis=0)

    def low_rows(slots, y):
        low = jnp.bitwise_and(spread(slots, y, LOW), LOW - 1)
        return jnp.where(low == row_low, 1.0, 0.0).astype(bf16)

    def add_row(sums, slots, fields, right, y):
        mask = lax.shift_right_logical(spread(slots, y, HIGH), 4) == row_high
        left = jnp.concatenate([jnp.where(mask, spread(field, y, HIGH), 0.0) for field in fields], axis=0)
        return sums + lax.dot_general(
            left.astype(bf16), right, (((1,), (1,)), ((), ())), preferred_element_type=f32
        )

    def split(high, low, weighted):
        upper = weighted.astype(bf16).astype(f32)
        high[...] = upper
        low[...] = weighted - upper

    for x in range(nx):
        here = cond[x]
        if x > 0:
            lx[x] = harmonic(cond[x - 1], here)
        right = jnp.where(lane == nz - 1, 0.0, harmonic(here, pltpu.roll(here, nz - 1, 1)))
        up = jnp.where(row == ny - 1, 0.0, harmonic(here, pltpu.roll(here, ny - 1, 0)))
        lz[x] = right
        lzleft[x] = pltpu.roll(right, 1, 1)
        ly[x] = up
        lydown[x] = pltpu.roll(up, 1, 0)
    for x in range(nx):
        phase = m[x]
        cap = jnp.where(phase == 0, 1.0, jnp.where(phase == 1, 2.0, 1.5)).astype(f32)
        whole = cap + lz[x] + lzleft[x] + ly[x] + lydown[x]
        if x > 0:
            whole = whole + lx[x]
        if x < nx - 1:
            whole = whole + lx[x + 1]
        diag[x] = whole

    def apply(field, x):
        v = field[x]
        out = diag[x] * v
        if x > 0:
            out = out - lx[x] * field[x - 1]
        if x < nx - 1:
            out = out - lx[x + 1] * field[x + 1]
        out = out - ly[x] * pltpu.roll(v, ny - 1, 0) - lydown[x] * pltpu.roll(v, 1, 0)
        return out - lz[x] * pltpu.roll(v, nz - 1, 1) - lzleft[x] * pltpu.roll(v, 1, 1)

    for x in range(nx):
        z1[x] = apply(r, x)

    def split_into(x, k, weighted):
        upper = weighted.astype(bf16).astype(f32)
        lower = weighted - upper
        for t in range(nz // SKETCH):
            at = slice(t * SKETCH, (t + 1) * SKETCH)
            parts[x, t, pl.ds(k, ny, stride=4), :] = upper[:, at]
            parts[x, t, pl.ds(k + 1, ny, stride=4), :] = lower[:, at]

    def masked(x, y):
        pair = jnp.concatenate([parts[x, t, pl.ds(y // 2 * 8, 8), :] for t in range(nz // SKETCH)], axis=1)
        swapped = pltpu.roll(pair, 4, 0)
        both = jnp.where(place < 4, pair, swapped) if y % 2 == 0 else jnp.where(place < 4, swapped, pair)
        return jnp.concatenate([both, both], axis=0).astype(bf16) * highs[x, y]

    def matmul(left, right):
        return lax.dot_general(left, right, (((1,), (1,)), ((), ())), preferred_element_type=f32)

    def begin_sketch(x, sums):
        split_into(x, 0, d[x] * r[x])
        split_into(x, 2, jnp.zeros((ny, nz), f32))
        for y in range(ny):
            low = jnp.bitwise_and(spread(slot.at[x], y, WIDE), WIDE - 1)
            right = jnp.where(low == row_wide, 1.0, 0.0).astype(bf16)
            onehot[x, y] = right
            high = lax.shift_right_logical(spread(slot.at[x], y, HIGH), 5)
            mask = [jnp.where(high == row_half + 2 * k, 1.0, 0.0) for k in (0, 1)]
            highs[x, y] = jnp.concatenate(mask, axis=0).astype(bf16)
            sums = sums + matmul(masked(x, y), right)
        return sums

    column = lax.broadcasted_iota(jnp.int32, (HIGH, SKETCH), 1)
    place_row = lax.broadcasted_iota(jnp.int32, (HIGH, SKETCH), 0)

    def padded(block):
        return jnp.concatenate([block, jnp.zeros((HIGH, SKETCH - block.shape[1]), f32)], axis=1)

    def turned(wide, rows, columns):
        wide = pltpu.roll(wide, rows % HIGH, 0) if rows % HIGH else wide
        return pltpu.roll(wide, columns % SKETCH, 1) if columns % SKETCH else wide

    def folded(sums, base, k):
        low, high = padded(sums[:HIGH]), padded(sums[HIGH:])
        low = turned(low + turned(low, -1, 0), -base, 0)
        high = turned(high + turned(high, -1, 0), -base, 0)
        quarter = jnp.bitwise_and(place_row, 3)
        even = turned(jnp.where(quarter == 0, low, turned(high, 2, 0)), 0, k * LOW)
        odd = turned(jnp.where(quarter == 1, turned(low, 1, 0), turned(high, 3, 0)), 0, (k - 1) * LOW)
        out = jnp.where(jnp.bitwise_and(place_row, 1) == 0, even, odd)
        return jnp.where(lax.div(column, LOW) == k, out, 0.0)

    mine[...] = folded(lax.fori_loop(0, nx, begin_sketch, jnp.zeros((2 * HIGH, WIDE), f32)), 0, 3)
    if ngy > 1:
        pl.when(middle)(functools.partial(pass_on, 1))
        pl.when(middle)(functools.partial(pass_on, 0))

    arrive_beside(near)
    arrive(0, hx_first, hy_first)
    for s in (0, 1):
        e = edge_x[s]
        link = harmonic(hx_first[s, 0], cond[e])
        lx[nx * s] = link
        z1[e] = z1[e] + link * (r[e] - hx_first[s, 1])
    for s in (0, 1):
        for x in range(nx):
            here, there = pl.ds(x, 1), pl.ds(nx + x, 1)
            link = harmonic(hy_first[s, there, :], py_first[s, there, :])
            lyb[s, here, :] = link
            flux = link * (py_first[s, here, :] - hy_first[s, here, :])
            after = z1[x, pl.ds(edge_y[s], 1), :] + flux
            z1[x, pl.ds(edge_y[s], 1), :] = after
            py_z[s, here, :] = after
    begin(2, lambda s: z1.at[edge_x[s]], hx_z, lambda s: py_z.at[s], hy_z)
    chains = [jnp.zeros((2 * HIGH, WIDE), f32) for _ in range(2)]
    for x in range(nx):
        out = apply(z1, x)
        for s in (0, 1):
            if x == edge_x[s]:
                out = out + lx[nx * s] * z1[x]
        z2[x] = out
        for s in (0, 1):
            at = (x, pl.ds(edge_y[s], 1), slice(None))
            z2[at] = z2[at] + lyb[s, pl.ds(x, 1), :] * py_z[s, pl.ds(x, 1), :]
        split_into(x, 0, d[x] * z1[x])
        split_into(x, 2, d[x] * z2[x])
        for y in range(ny):
            chains[y % 2] = chains[y % 2] + matmul(masked(x, y), onehot[x, y])
    edge_chains = [jnp.zeros((2 * HIGH, LOW), f32) for _ in range(2)]

    def sketch_edge(t, rows):
        for y in range(rows):
            onehot_edge[t, y] = low_rows(sedge.at[t], y)
        for y in range(rows):
            edge_chains[y % 2] = add_row(
                edge_chains[y % 2], sedge.at[t], (wedge.at[0, t], wedge.at[1, t]), onehot_edge[t, y], y
            )

    def face_edge(t, side):
        split(wedge.at[0, t], wedge.at[1, t], -lx[nx * side] * z1[(nx - 1) * side] * hx_early[side, 1])
        sedge[t] = hx_early[side, 0].astype(jnp.int32)
        sketch_edge(t, ny)

    face_edge(0, near)
    settle(1, has_y, arrival(1, 1, 0), hy_early, "wait_recv")
    for s in (0, 1):
        for x in range(nx):
            at = pl.ds(s * nx + x, 1)
            edge = -lyb[s, pl.ds(x, 1), :] * py_z[s, pl.ds(x, 1), :] * hy_early[s, pl.ds(nx + x, 1), :]
            upper = edge.astype(bf16).astype(f32)
            wedge[0, 1, at, :] = upper
            wedge[1, 1, at, :] = edge - upper
            sedge[1, at, :] = hy_early[s, pl.ds(x, 1), :].astype(jnp.int32)
    sketch_edge(1, 2 * nx)
    arrive_beside(far)
    face_edge(2, far)
    out = mine[...]
    for sums, edge_sums in zip(chains, edge_chains):
        out = out + folded(sums, 0, 1) + folded(sums, 2, 2)
        out = out + padded(edge_sums[:HIGH] + edge_sums[HIGH:])
    mine[...] = out

    def share(step, carry):
        pltpu.make_async_remote_copy(
            src_ref=mine,
            dst_ref=gathered.at[me],
            send_sem=share_sem.at[0],
            recv_sem=share_sem.at[1],
            device_id=peer(step),
            device_id_type=MESH,
        ).start()
        return carry

    for s in (0, 1):

        @pl.when(jnp.logical_and(has_y[1 - s], jnp.logical_not(has_y[s])))
        def _():
            pl.semaphore_wait(known.at[s], 1)

    lax.fori_loop(0, count - 1, share, 0)
    gathered[me] = mine[...]
    arrive(2, hx_z, hy_z)
    for s in (0, 1):
        z2[edge_x[s]] = z2[edge_x[s]] - lx[nx * s] * hx_z[s]
        for x in range(nx):
            at = (x, pl.ds(edge_y[s], 1), slice(None))
            z2[at] = z2[at] - lyb[s, pl.ds(x, 1), :] * hy_z[s, pl.ds(x, 1), :]
    others = gathered.at[pl.ds(0, count - 1)]
    shared = pltpu.make_async_remote_copy(
        src_ref=others,
        dst_ref=others,
        send_sem=share_sem.at[0],
        recv_sem=share_sem.at[1],
        device_id=peer(0),
        device_id_type=MESH,
    )
    shared.wait_recv()
    summed = jnp.sum(gathered[...], axis=0)
    first_lanes = lax.broadcasted_iota(jnp.int32, (HIGH, SKETCH), 1) < LOW
    s0, s1, s2 = (jnp.where(first_lanes, pltpu.roll(summed, SKETCH - k * LOW, 1), 0.0) for k in (3, 1, 2))
    c0, c1 = coefficients(s0, s1, s2 + jnp.where(first_lanes, summed, 0.0))
    for x in range(nx):
        answer[x] = c0 * r[x] + c1 * z1[x]
        rest[x] = r[x] - c0 * z1[x] - c1 * z2[x]
    shared.wait_send()
    settle(0, has_x, sent.at[0], bulk_x, "wait_send")
    settle(1, has_y, sent.at[1], bulk_y, "wait_send")


def put_out(answer, rest, answer_out, rest_out, sem):
    one = pltpu.make_async_copy(answer, answer_out, sem.at[0])
    two = pltpu.make_async_copy(rest, rest_out, sem.at[1])
    one.start()
    two.start()
    one.wait()
    two.wait()


def body(ngx, ngy, f, w, m, s, d):
    nx, ny, nz = f.shape
    count = ngx * ngy
    vm = lambda shape, dtype=f32: pltpu.VMEM(shape, dtype)
    block = (nx, ny, nz)
    assert 2 * nx <= ny and nx % 2 == 0
    answer, rest = pl.pallas_call(
        functools.partial(kernel, ngx, ngy, nx, ny, nz),
        out_shape=(vm(block), vm(block)),
        in_specs=[pl.BlockSpec(memory_space=pl.ANY)] * 5,
        out_specs=[pl.BlockSpec(memory_space=pltpu.VMEM)] * 2,
        scratch_shapes=[
            vm(block), vm(block),
            vm(block), vm(block), vm(block, jnp.int32), vm(block, jnp.int32), vm(block),
            vm(block), vm(block),
            vm((nx + 1, ny, nz)), vm(block), vm(block), vm(block), vm(block), vm((2, nx, nz)),
            vm((nx, ny, WIDE, nz), bf16), vm((nx, ny, 2 * HIGH, nz), bf16), vm((3, ny, LOW, nz), bf16), vm((nx, nz // SKETCH, 4 * ny, SKETCH)), vm((2, 3, ny, nz)), vm((3, ny, nz), jnp.int32),
            vm((2, 2, ny, nz)), vm((2, 2, ny, nz)), vm((2, ny, nz)), vm((2, 2 * nx, nz)), vm((2, 2 * nx, nz)), vm((2, nx, nz)),
            vm((2, 2, ny, nz)), vm((2, 2, ny, nz)), vm((2, 2 * nx, nz)), vm((2, 2 * nx, nz)), vm((2, nx, nz)),
            vm((2, 5, ny, nz)), vm((2, 5, nx, nz)),
            vm((HIGH, SKETCH)), vm((count, HIGH, SKETCH)),
            pltpu.SemaphoreType.DMA((3,)),
            pltpu.SemaphoreType.DMA((2,)),
            pltpu.SemaphoreType.DMA((5,)),
            pltpu.SemaphoreType.DMA((2,)),
            pltpu.SemaphoreType.DMA((2,)),
            pltpu.SemaphoreType.REGULAR((2,)),
        ],
        compiler_params=pltpu.CompilerParams(collective_id=0, has_side_effects=True),
        name="sketched_gmres",
    )(f, w, m, s, d)
    return pl.pallas_call(
        put_out,
        out_shape=(jax.ShapeDtypeStruct(block, f32), jax.ShapeDtypeStruct(block, f32)),
        in_specs=[pl.BlockSpec(memory_space=pltpu.VMEM)] * 2,
        out_specs=[pl.BlockSpec(memory_space=pl.ANY)] * 2,
        scratch_shapes=[pltpu.SemaphoreType.DMA((2,))],
        name="put_out",
    )(pltpu.with_memory_space_constraint(answer, pltpu.VMEM), pltpu.with_memory_space_constraint(rest, pltpu.VMEM))


def solution(mesh):
    spec = P(("parts", "gx"), "gy", None)
    return jax.shard_map(
        functools.partial(body, mesh.shape["gx"], mesh.shape["gy"]),
        mesh=mesh,
        in_specs=(spec,) * 5,
        out_specs=(spec, spec),
        check_vma=False,
    )
```

```python
import functools

import jax
import jax.numpy as jnp
from jax import lax
from jax.experimental import pallas as pl
from jax.experimental.pallas import tpu as pltpu
from jax.sharding import PartitionSpec as P

SKETCH = 128
LOW = 16
HIGH = SKETCH // LOW
WIDE = 32
MESH = pl.DeviceIdType.MESH
epsilon = 1e-06
highest = lax.Precision.HIGHEST
f32 = jnp.float32
bf16 = jnp.bfloat16


def harmonic(first, second):
    return 2.0 * first * second / (first + second)


def total(field):
    return jnp.sum(jnp.sum(field, axis=1, keepdims=True), axis=0, keepdims=True)


def coefficients(s0, s1, s2):
    inv_beta2 = 1.0 / (total(s0 * s0) + epsilon)
    h00 = total(s0 * s1) * inv_beta2
    t0 = s1 - h00 * s0
    w1 = s2 - h00 * s1
    n0sq = total(t0 * t0) * inv_beta2 + epsilon
    cross = total(s0 * w1) * inv_beta2
    along = total(t0 * w1) * inv_beta2
    whole = total(w1 * w1) * inv_beta2
    inv_n0sq = 1.0 / n0sq
    h11 = along * inv_n0sq
    shift = epsilon * inv_beta2
    left = whole - cross * cross * (1.0 + shift) - h11 * h11 * (n0sq + epsilon) + 2.0 * cross * h11 * h00 * shift
    n1sq = jnp.maximum(left, 0.0) * inv_n0sq + epsilon
    minor = h00 * h11 - cross
    inv_det = 1.0 / (minor * minor + n1sq * (h00 * h00 + n0sq))
    return (minor * (h11 + h00) + h00 * n1sq) * inv_det, -minor * inv_det


def kernel(
    ngx, ngy, nx, ny, nz,
    f_hbm, w_hbm, m_hbm, s_hbm, d_hbm,
    kept,
    z1, z2, r, w, m, slot, d, cond, diag, lx, ly, lydown, lz, lzleft, lyb, onehot, highs, onehot_edge, parts, wedge, sedge,
    hx_first, hx_early, hx_z, hy_first, hy_early, hy_z,
    px_first, px_early, py_first, py_early, py_z,
    bulk_x, bulk_y, mine, gathered, load_sem, sent, landed, beside, share_sem, known,
):
    gx = lax.axis_index("gx")
    gy = lax.axis_index("gy")
    count = ngx * ngy
    me = gx * ngy + gy


    mine_at = gy * ngx + gx

    def peer(step):
        other = step + (step >= mine_at).astype(jnp.int32)
        return {"gx": lax.rem(other, ngx), "gy": lax.div(other, ngx)}

    barrier = pltpu.get_barrier_semaphore()

    has_x = (gx > 0, gx < ngx - 1)
    has_y = (gy > 0, gy < ngy - 1)
    to_x = ({"gx": gx - 1, "gy": gy}, {"gx": gx + 1, "gy": gy})
    to_y = ({"gx": gx, "gy": gy - 1}, {"gx": gx, "gy": gy + 1})
    for s in (0, 1):

        @pl.when(has_y[s])
        def _():
            pl.semaphore_signal(barrier, inc=1, device_id=to_y[s], device_id_type=MESH)

    for step in range(1, ngx):
        other = {"gx": lax.rem(gx + step, ngx), "gy": gy}
        pl.semaphore_signal(barrier, inc=1, device_id=other, device_id_type=MESH)

    loads = [
        pltpu.make_async_copy(src, dst, load_sem.at[i])
        for i, src, dst in ((0, w_hbm, w), (0, m_hbm, m), (0, f_hbm, r), (1, s_hbm, slot), (1, d_hbm, d))
    ]
    for load in loads:
        load.start()

    n_y = has_y[0].astype(jnp.int32) + has_y[1].astype(jnp.int32)

    def tell(side):
        pl.semaphore_signal(known.at[side], inc=1, device_id=to_y[side], device_id_type=MESH)

    def pass_on(side):
        pl.semaphore_wait(known.at[side], 1)
        tell(side)

    middle = jnp.logical_and(has_y[0], has_y[1])

    edge_x = (0, nx - 1)
    edge_y = (0, ny - 1)

    def arrival(axis, index, side):
        if axis == 0 and index == 1:
            return beside.at[side]
        return landed.at[(0, None, 1)[index] if axis == 0 else 2 + index]

    def remote(src, dst, axis, index, side, target):
        return pltpu.make_async_remote_copy(
            src_ref=src,
            dst_ref=dst.at[1 - side],
            send_sem=sent.at[axis],
            recv_sem=arrival(axis, index, 1 - side),
            device_id=target,
            device_id_type=MESH,
        )

    def begin(index, src_x, dst_x, src_y, dst_y):
        for s in (0, 1):
            pl.when(has_y[s])(remote(src_y(s), dst_y, 1, index, s, to_y[s]).start)
        for s in (0, 1):
            pl.when(has_x[s])(remote(src_x(s), dst_x, 0, index, s, to_x[s]).start)

    def settle(axis, has, sem, ref, kind):
        target = to_x[0] if axis == 0 else to_y[0]

        def wait(part):
            copy = pltpu.make_async_remote_copy(
                src_ref=part, dst_ref=part, send_sem=sem, recv_sem=sem, device_id=target, device_id_type=MESH
            )
            return getattr(copy, kind)

        pl.when(jnp.logical_and(has[0], has[1]))(wait(ref))
        pl.when(jnp.logical_xor(has[0], has[1]))(wait(ref.at[0]))

    def arrive(index, dst_x, dst_y):
        settle(0, has_x, arrival(0, index, 0), dst_x, "wait_recv")
        settle(1, has_y, arrival(1, index, 0), dst_y, "wait_recv")

    far = jnp.bitwise_and(gx, 1)
    near = 1 - far

    def arrive_beside(side):
        copy = pltpu.make_async_remote_copy(
            src_ref=hx_early.at[side],
            dst_ref=hx_early.at[side],
            send_sem=sent.at[0],
            recv_sem=beside.at[side],
            device_id=to_x[0],
            device_id_type=MESH,
        )
        pl.when(jnp.logical_or(jnp.logical_and(side == 0, has_x[0]), jnp.logical_and(side == 1, has_x[1])))(copy.wait_recv)

    def loaded(i, blocks):
        size = parts.at[pl.ds(0, blocks * nx // 4)]
        pltpu.make_async_copy(size, size, load_sem.at[i]).wait()

    loaded(0, 3)
    for x in range(nx):
        phase = m[x]
        cond[x] = jnp.where(phase == 0, 0.2, jnp.where(phase == 1, 1.0, 0.6)).astype(f32) * (0.5 + w[x])
    for s in (0, 1):
        e = edge_x[s]
        px_first[s, 0] = cond[e]
        px_first[s, 1] = r[e]
        for x in range(nx):
            py_first[s, pl.ds(x, 1), :] = r[x, pl.ds(edge_y[s], 1), :]
            py_first[s, pl.ds(nx + x, 1), :] = cond[x, pl.ds(edge_y[s], 1), :]

    pl.semaphore_wait(barrier, ngx - 1 + n_y)
    begin(0, lambda s: px_first.at[s], hx_first, lambda s: py_first.at[s], hy_first)
    if ngy > 1:
        pl.when(gy == 0)(functools.partial(tell, 1))
        pl.when(gy == ngy - 1)(functools.partial(tell, 0))
    loaded(1, 2)
    for s in (0, 1):
        e = edge_x[s]
        px_early[s, 0] = slot[e].astype(f32)
        px_early[s, 1] = d[e]
        for x in range(nx):
            py_early[s, pl.ds(x, 1), :] = slot[x, pl.ds(edge_y[s], 1), :].astype(f32)
            py_early[s, pl.ds(nx + x, 1), :] = d[x, pl.ds(edge_y[s], 1), :]
    begin(1, lambda s: px_early.at[s], hx_early, lambda s: py_early.at[s], hy_early)

    for s in (0, 1):

        @pl.when(jnp.logical_not(has_x[s]))
        def _():
            hx_first[s] = jnp.zeros((2, ny, nz), f32)
            hx_early[s] = jnp.zeros((2, ny, nz), f32)
            hx_z[s] = jnp.zeros((ny, nz), f32)

        @pl.when(jnp.logical_not(has_y[s]))
        def _():
            hy_first[s] = jnp.zeros((2 * nx, nz), f32)
            hy_early[s] = jnp.zeros((2 * nx, nz), f32)
            hy_z[s] = jnp.zeros((nx, nz), f32)

    lane = lax.broadcasted_iota(jnp.int32, (ny, nz), 1)
    row = lax.broadcasted_iota(jnp.int32, (ny, nz), 0)
    place = lax.broadcasted_iota(jnp.int32, (HIGH, nz), 0)
    row_half = lax.shift_right_logical(place, 2)
    row_high = 2 * row_half + 4 * jnp.bitwise_and(lax.shift_right_logical(place, 1), 1) + jnp.bitwise_and(place, 1)
    row_low = lax.broadcasted_iota(jnp.int32, (LOW, nz), 0)
    row_wide = lax.broadcasted_iota(jnp.int32, (WIDE, nz), 0)

    def spread(ref, y, rows):
        part = ref[pl.ds(y, 8, stride=0), :]
        return part if rows == 8 else jnp.concatenate([part] * (rows // 8), axis=0)

    def low_rows(slots, y):
        low = jnp.bitwise_and(spread(slots, y, LOW), LOW - 1)
        return jnp.where(low == row_low, 1.0, 0.0).astype(bf16)

    def add_row(sums, slots, fields, right, y):
        mask = lax.shift_right_logical(spread(slots, y, HIGH), 4) == row_high
        left = jnp.concatenate([jnp.where(mask, spread(field, y, HIGH), 0.0) for field in fields], axis=0)
        return sums + lax.dot_general(
            left.astype(bf16), right, (((1,), (1,)), ((), ())), preferred_element_type=f32
        )

    def split(high, low, weighted):
        upper = weighted.astype(bf16).astype(f32)
        high[...] = upper
        low[...] = weighted - upper

    for x in range(nx):
        here = cond[x]
        if x > 0:
            lx[x] = harmonic(cond[x - 1], here)
        right = jnp.where(lane == nz - 1, 0.0, harmonic(here, pltpu.roll(here, nz - 1, 1)))
        up = jnp.where(row == ny - 1, 0.0, harmonic(here, pltpu.roll(here, ny - 1, 0)))
        lz[x] = right
        lzleft[x] = pltpu.roll(right, 1, 1)
        ly[x] = up
        lydown[x] = pltpu.roll(up, 1, 0)
    for x in range(nx):
        phase = m[x]
        cap = jnp.where(phase == 0, 1.0, jnp.where(phase == 1, 2.0, 1.5)).astype(f32)
        whole = cap + lz[x] + lzleft[x] + ly[x] + lydown[x]
        if x > 0:
            whole = whole + lx[x]
        if x < nx - 1:
            whole = whole + lx[x + 1]
        diag[x] = whole

    def apply(field, x):
        v = field[x]
        out = diag[x] * v
        if x > 0:
            out = out - lx[x] * field[x - 1]
        if x < nx - 1:
            out = out - lx[x + 1] * field[x + 1]
        out = out - ly[x] * pltpu.roll(v, ny - 1, 0) - lydown[x] * pltpu.roll(v, 1, 0)
        return out - lz[x] * pltpu.roll(v, nz - 1, 1) - lzleft[x] * pltpu.roll(v, 1, 1)

    for x in range(nx):
        z1[x] = apply(r, x)

    def split_into(x, k, weighted):
        upper = weighted.astype(bf16).astype(f32)
        lower = weighted - upper
        for t in range(nz // SKETCH):
            at = slice(t * SKETCH, (t + 1) * SKETCH)
            parts[x, t, pl.ds(k, ny, stride=4), :] = upper[:, at]
            parts[x, t, pl.ds(k + 1, ny, stride=4), :] = lower[:, at]

    def masked(x, y):
        pair = jnp.concatenate([parts[x, t, pl.ds(y // 2 * 8, 8), :] for t in range(nz // SKETCH)], axis=1)
        swapped = pltpu.roll(pair, 4, 0)
        both = jnp.where(place < 4, pair, swapped) if y % 2 == 0 else jnp.where(place < 4, swapped, pair)
        return jnp.concatenate([both, both], axis=0).astype(bf16) * highs[x, y]

    def matmul(left, right):
        return lax.dot_general(left, right, (((1,), (1,)), ((), ())), preferred_element_type=f32)

    def begin_sketch(x, sums):
        split_into(x, 0, d[x] * r[x])
        split_into(x, 2, jnp.zeros((ny, nz), f32))
        for y in range(ny):
            low = jnp.bitwise_and(spread(slot.at[x], y, WIDE), WIDE - 1)
            right = jnp.where(low == row_wide, 1.0, 0.0).astype(bf16)
            onehot[x, y] = right
            high = lax.shift_right_logical(spread(slot.at[x], y, HIGH), 5)
            mask = [jnp.where(high == row_half + 2 * k, 1.0, 0.0) for k in (0, 1)]
            highs[x, y] = jnp.concatenate(mask, axis=0).astype(bf16)
            sums = sums + matmul(masked(x, y), right)
        return sums

    column = lax.broadcasted_iota(jnp.int32, (HIGH, SKETCH), 1)
    place_row = lax.broadcasted_iota(jnp.int32, (HIGH, SKETCH), 0)

    def padded(block):
        return jnp.concatenate([block, jnp.zeros((HIGH, SKETCH - block.shape[1]), f32)], axis=1)

    def turned(wide, rows, columns):
        wide = pltpu.roll(wide, rows % HIGH, 0) if rows % HIGH else wide
        return pltpu.roll(wide, columns % SKETCH, 1) if columns % SKETCH else wide

    def folded(sums, base, k):
        low, high = padded(sums[:HIGH]), padded(sums[HIGH:])
        low = turned(low + turned(low, -1, 0), -base, 0)
        high = turned(high + turned(high, -1, 0), -base, 0)
        quarter = jnp.bitwise_and(place_row, 3)
        even = turned(jnp.where(quarter == 0, low, turned(high, 2, 0)), 0, k * LOW)
        odd = turned(jnp.where(quarter == 1, turned(low, 1, 0), turned(high, 3, 0)), 0, (k - 1) * LOW)
        out = jnp.where(jnp.bitwise_and(place_row, 1) == 0, even, odd)
        return jnp.where(lax.div(column, LOW) == k, out, 0.0)

    mine[...] = folded(lax.fori_loop(0, nx, begin_sketch, jnp.zeros((2 * HIGH, WIDE), f32)), 0, 3)
    if ngy > 1:
        pl.when(middle)(functools.partial(pass_on, 1))
        pl.when(middle)(functools.partial(pass_on, 0))

    def place_edge(t, rows):
        for y in range(rows):
            onehot_edge[t, y] = low_rows(sedge.at[t], y)

    arrive_beside(near)
    sedge[0] = hx_early[near, 0].astype(jnp.int32)
    place_edge(0, ny)
    arrive(0, hx_first, hy_first)
    for s in (0, 1):
        e = edge_x[s]
        link = harmonic(hx_first[s, 0], cond[e])
        lx[nx * s] = link
        z1[e] = z1[e] + link * (r[e] - hx_first[s, 1])
    for s in (0, 1):
        for x in range(nx):
            here, there = pl.ds(x, 1), pl.ds(nx + x, 1)
            link = harmonic(hy_first[s, there, :], py_first[s, there, :])
            lyb[s, here, :] = link
            flux = link * (py_first[s, here, :] - hy_first[s, here, :])
            after = z1[x, pl.ds(edge_y[s], 1), :] + flux
            z1[x, pl.ds(edge_y[s], 1), :] = after
            py_z[s, here, :] = after
    begin(2, lambda s: z1.at[edge_x[s]], hx_z, lambda s: py_z.at[s], hy_z)
    chains = [jnp.zeros((2 * HIGH, WIDE), f32) for _ in range(2)]
    for x in range(nx):
        out = apply(z1, x)
        for s in (0, 1):
            if x == edge_x[s]:
                out = out + lx[nx * s] * z1[x]
        z2[x] = out
        for s in (0, 1):
            at = (x, pl.ds(edge_y[s], 1), slice(None))
            z2[at] = z2[at] + lyb[s, pl.ds(x, 1), :] * py_z[s, pl.ds(x, 1), :]
        split_into(x, 0, d[x] * z1[x])
        split_into(x, 2, d[x] * z2[x])
        for y in range(ny):
            chains[y % 2] = chains[y % 2] + matmul(masked(x, y), onehot[x, y])
    edge_chains = [jnp.zeros((2 * HIGH, LOW), f32) for _ in range(2)]

    def sketch_edge(t, rows):
        for y in range(rows):
            edge_chains[y % 2] = add_row(
                edge_chains[y % 2], sedge.at[t], (wedge.at[0, t], wedge.at[1, t]), onehot_edge[t, y], y
            )

    def weigh_face(t, side):
        split(wedge.at[0, t], wedge.at[1, t], -lx[nx * side] * z1[(nx - 1) * side] * hx_early[side, 1])

    weigh_face(0, near)
    sketch_edge(0, ny)
    settle(1, has_y, arrival(1, 1, 0), hy_early, "wait_recv")
    for s in (0, 1):
        for x in range(nx):
            at = pl.ds(s * nx + x, 1)
            edge = -lyb[s, pl.ds(x, 1), :] * py_z[s, pl.ds(x, 1), :] * hy_early[s, pl.ds(nx + x, 1), :]
            upper = edge.astype(bf16).astype(f32)
            wedge[0, 1, at, :] = upper
            wedge[1, 1, at, :] = edge - upper
            sedge[1, at, :] = hy_early[s, pl.ds(x, 1), :].astype(jnp.int32)
    place_edge(1, 2 * nx)
    sketch_edge(1, 2 * nx)
    arrive_beside(far)
    sedge[2] = hx_early[far, 0].astype(jnp.int32)
    place_edge(2, ny)
    weigh_face(2, far)
    sketch_edge(2, ny)
    out = mine[...]
    for sums, edge_sums in zip(chains, edge_chains):
        out = out + folded(sums, 0, 1) + folded(sums, 2, 2)
        out = out + padded(edge_sums[:HIGH] + edge_sums[HIGH:])
    mine[...] = out

    def share(step, carry):
        pltpu.make_async_remote_copy(
            src_ref=mine,
            dst_ref=gathered.at[me],
            send_sem=share_sem.at[0],
            recv_sem=share_sem.at[1],
            device_id=peer(step),
            device_id_type=MESH,
        ).start()
        return carry

    for s in (0, 1):

        @pl.when(jnp.logical_and(has_y[1 - s], jnp.logical_not(has_y[s])))
        def _():
            pl.semaphore_wait(known.at[s], 1)

    lax.fori_loop(0, count - 1, share, 0)
    gathered[me] = mine[...]
    arrive(2, hx_z, hy_z)
    for s in (0, 1):
        z2[edge_x[s]] = z2[edge_x[s]] - lx[nx * s] * hx_z[s]
        for x in range(nx):
            at = (x, pl.ds(edge_y[s], 1), slice(None))
            z2[at] = z2[at] - lyb[s, pl.ds(x, 1), :] * hy_z[s, pl.ds(x, 1), :]
    others = gathered.at[pl.ds(0, count - 1)]
    shared = pltpu.make_async_remote_copy(
        src_ref=others,
        dst_ref=others,
        send_sem=share_sem.at[0],
        recv_sem=share_sem.at[1],
        device_id=peer(0),
        device_id_type=MESH,
    )
    shared.wait_recv()
    summed = jnp.sum(gathered[...], axis=0)
    first_lanes = lax.broadcasted_iota(jnp.int32, (HIGH, SKETCH), 1) < LOW
    s0, s1, s2 = (jnp.where(first_lanes, pltpu.roll(summed, SKETCH - k * LOW, 1), 0.0) for k in (3, 1, 2))
    c0, c1 = coefficients(s0, s1, s2 + jnp.where(first_lanes, summed, 0.0))
    for x in range(nx):
        kept[0, x] = c0 * r[x] + c1 * z1[x]
        kept[1, x] = r[x] - c0 * z1[x] - c1 * z2[x]
    shared.wait_send()
    settle(0, has_x, sent.at[0], bulk_x, "wait_send")
    settle(1, has_y, sent.at[1], bulk_y, "wait_send")


def put_out(kept, answer_out, rest_out, sem):
    pltpu.make_async_copy(kept.at[0], answer_out, sem.at[0]).start()
    pltpu.make_async_copy(kept.at[1], rest_out, sem.at[0]).start()
    pltpu.make_async_copy(kept, kept, sem.at[0]).wait()


def body(ngx, ngy, f, w, m, s, d):
    nx, ny, nz = f.shape
    count = ngx * ngy
    vm = lambda shape, dtype=f32: pltpu.VMEM(shape, dtype)
    block = (nx, ny, nz)
    assert 2 * nx <= ny and nx % 4 == 0
    kept = pl.pallas_call(
        functools.partial(kernel, ngx, ngy, nx, ny, nz),
        out_shape=vm((2,) + block),
        in_specs=[pl.BlockSpec(memory_space=pl.ANY)] * 5,
        out_specs=pl.BlockSpec(memory_space=pltpu.VMEM),
        scratch_shapes=[
            vm(block), vm(block),
            vm(block), vm(block), vm(block, jnp.int32), vm(block, jnp.int32), vm(block),
            vm(block), vm(block),
            vm((nx + 1, ny, nz)), vm(block), vm(block), vm(block), vm(block), vm((2, nx, nz)),
            vm((nx, ny, WIDE, nz), bf16), vm((nx, ny, 2 * HIGH, nz), bf16), vm((3, ny, LOW, nz), bf16), vm((nx, nz // SKETCH, 4 * ny, SKETCH)), vm((2, 3, ny, nz)), vm((3, ny, nz), jnp.int32),
            vm((2, 2, ny, nz)), vm((2, 2, ny, nz)), vm((2, ny, nz)), vm((2, 2 * nx, nz)), vm((2, 2 * nx, nz)), vm((2, nx, nz)),
            vm((2, 2, ny, nz)), vm((2, 2, ny, nz)), vm((2, 2 * nx, nz)), vm((2, 2 * nx, nz)), vm((2, nx, nz)),
            vm((2, 5, ny, nz)), vm((2, 5, nx, nz)),
            vm((HIGH, SKETCH)), vm((count, HIGH, SKETCH)),
            pltpu.SemaphoreType.DMA((2,)),
            pltpu.SemaphoreType.DMA((2,)),
            pltpu.SemaphoreType.DMA((5,)),
            pltpu.SemaphoreType.DMA((2,)),
            pltpu.SemaphoreType.DMA((2,)),
            pltpu.SemaphoreType.REGULAR((2,)),
        ],
        compiler_params=pltpu.CompilerParams(collective_id=0, has_side_effects=True),
        name="sketched_gmres",
    )(f, w, m, s, d)
    return pl.pallas_call(
        put_out,
        out_shape=(jax.ShapeDtypeStruct(block, f32), jax.ShapeDtypeStruct(block, f32)),
        in_specs=[pl.BlockSpec(memory_space=pltpu.VMEM)],
        out_specs=[pl.BlockSpec(memory_space=pl.ANY)] * 2,
        scratch_shapes=[pltpu.SemaphoreType.DMA((1,))],
        name="put_out",
    )(pltpu.with_memory_space_constraint(kept, pltpu.VMEM))


def solution(mesh):
    spec = P(("parts", "gx"), "gy", None)
    return jax.shard_map(
        functools.partial(body, mesh.shape["gx"], mesh.shape["gy"]),
        mesh=mesh,
        in_specs=(spec,) * 5,
        out_specs=(spec, spec),
        check_vma=False,
    )
```

```python
import functools

import jax
import jax.numpy as jnp
from jax import lax
from jax.experimental import pallas as pl
from jax.experimental.pallas import tpu as pltpu
from jax.sharding import PartitionSpec as P

SKETCH = 128
LOW = 16
HIGH = SKETCH // LOW
WIDE = 32
MESH = pl.DeviceIdType.MESH
epsilon = 1e-06
highest = lax.Precision.HIGHEST
f32 = jnp.float32
bf16 = jnp.bfloat16


def harmonic(first, second):
    return 2.0 * first * second / (first + second)


def total(field):
    return jnp.sum(jnp.sum(field, axis=1, keepdims=True), axis=0, keepdims=True)


def coefficients(s0, s1, s2):
    inv_beta2 = 1.0 / (total(s0 * s0) + epsilon)
    h00 = total(s0 * s1) * inv_beta2
    t0 = s1 - h00 * s0
    w1 = s2 - h00 * s1
    n0sq = total(t0 * t0) * inv_beta2 + epsilon
    cross = total(s0 * w1) * inv_beta2
    along = total(t0 * w1) * inv_beta2
    whole = total(w1 * w1) * inv_beta2
    inv_n0sq = 1.0 / n0sq
    h11 = along * inv_n0sq
    shift = epsilon * inv_beta2
    left = whole - cross * cross * (1.0 + shift) - h11 * h11 * (n0sq + epsilon) + 2.0 * cross * h11 * h00 * shift
    n1sq = jnp.maximum(left, 0.0) * inv_n0sq + epsilon
    minor = h00 * h11 - cross
    inv_det = 1.0 / (minor * minor + n1sq * (h00 * h00 + n0sq))
    return (minor * (h11 + h00) + h00 * n1sq) * inv_det, -minor * inv_det


def kernel(
    ngx, ngy, nx, ny, nz,
    f_hbm, w_hbm, m_hbm, s_hbm, d_hbm,
    answer, rest,
    z1, z2, r, w, m, slot, d, cond, diag, lx, ly, lydown, lz, lzleft, lyb, onehot, highs, onehot_edge, parts, wedge, sedge,
    hx_first, hx_early, hx_z, hy_first, hy_early, hy_z,
    px_first, px_early, py_first, py_early, py_z,
    bulk_x, bulk_y, mine, gathered, load_sem, sent, landed, beside, share_sem, known,
):
    gx = lax.axis_index("gx")
    gy = lax.axis_index("gy")
    count = ngx * ngy
    me = gx * ngy + gy


    mine_at = gy * ngx + gx

    def peer(step):
        other = step + (step >= mine_at).astype(jnp.int32)
        return {"gx": lax.rem(other, ngx), "gy": lax.div(other, ngx)}

    barrier = pltpu.get_barrier_semaphore()

    has_x = (gx > 0, gx < ngx - 1)
    has_y = (gy > 0, gy < ngy - 1)
    to_x = ({"gx": gx - 1, "gy": gy}, {"gx": gx + 1, "gy": gy})
    to_y = ({"gx": gx, "gy": gy - 1}, {"gx": gx, "gy": gy + 1})
    for s in (0, 1):

        @pl.when(has_y[s])
        def _():
            pl.semaphore_signal(barrier, inc=1, device_id=to_y[s], device_id_type=MESH)

    for step in range(1, ngx):
        other = {"gx": lax.rem(gx + step, ngx), "gy": gy}
        pl.semaphore_signal(barrier, inc=1, device_id=other, device_id_type=MESH)

    loads = [
        pltpu.make_async_copy(src, dst, load_sem.at[i])
        for i, src, dst in ((0, w_hbm, w), (0, m_hbm, m), (1, f_hbm, r), (2, s_hbm, slot), (2, d_hbm, d))
    ]
    for load in loads:
        load.start()

    n_y = has_y[0].astype(jnp.int32) + has_y[1].astype(jnp.int32)

    def tell(side):
        pl.semaphore_signal(known.at[side], inc=1, device_id=to_y[side], device_id_type=MESH)

    def pass_on(side):
        pl.semaphore_wait(known.at[side], 1)
        tell(side)

    middle = jnp.logical_and(has_y[0], has_y[1])

    edge_x = (0, nx - 1)
    edge_y = (0, ny - 1)

    def arrival(axis, index, side):
        if axis == 0 and index == 1:
            return beside.at[side]
        return landed.at[(0, None, 1)[index] if axis == 0 else 2 + index]

    def remote(src, dst, axis, index, side, target):
        return pltpu.make_async_remote_copy(
            src_ref=src,
            dst_ref=dst.at[1 - side],
            send_sem=sent.at[axis],
            recv_sem=arrival(axis, index, 1 - side),
            device_id=target,
            device_id_type=MESH,
        )

    def begin(index, src_x, dst_x, src_y, dst_y):
        for s in (0, 1):
            pl.when(has_y[s])(remote(src_y(s), dst_y, 1, index, s, to_y[s]).start)
        for s in (0, 1):
            pl.when(has_x[s])(remote(src_x(s), dst_x, 0, index, s, to_x[s]).start)

    def settle(axis, has, sem, ref, kind):
        target = to_x[0] if axis == 0 else to_y[0]

        def wait(part):
            copy = pltpu.make_async_remote_copy(
                src_ref=part, dst_ref=part, send_sem=sem, recv_sem=sem, device_id=target, device_id_type=MESH
            )
            return getattr(copy, kind)

        pl.when(jnp.logical_and(has[0], has[1]))(wait(ref))
        pl.when(jnp.logical_xor(has[0], has[1]))(wait(ref.at[0]))

    def arrive(index, dst_x, dst_y):
        settle(0, has_x, arrival(0, index, 0), dst_x, "wait_recv")
        settle(1, has_y, arrival(1, index, 0), dst_y, "wait_recv")

    far = jnp.bitwise_and(gx, 1)
    near = 1 - far

    def arrive_beside(side):
        copy = pltpu.make_async_remote_copy(
            src_ref=hx_early.at[side],
            dst_ref=hx_early.at[side],
            send_sem=sent.at[0],
            recv_sem=beside.at[side],
            device_id=to_x[0],
            device_id_type=MESH,
        )
        pl.when(jnp.logical_or(jnp.logical_and(side == 0, has_x[0]), jnp.logical_and(side == 1, has_x[1])))(copy.wait_recv)

    two_blocks = parts.at[pl.ds(0, nx // 2)]

    def both_loaded(i):
        pltpu.make_async_copy(two_blocks, two_blocks, load_sem.at[i]).wait()

    both_loaded(0)
    for x in range(nx):
        phase = m[x]
        cond[x] = jnp.where(phase == 0, 0.2, jnp.where(phase == 1, 1.0, 0.6)).astype(f32) * (0.5 + w[x])
    loads[2].wait()
    for s in (0, 1):
        e = edge_x[s]
        px_first[s, 0] = cond[e]
        px_first[s, 1] = r[e]
        for x in range(nx):
            py_first[s, pl.ds(x, 1), :] = r[x, pl.ds(edge_y[s], 1), :]
            py_first[s, pl.ds(nx + x, 1), :] = cond[x, pl.ds(edge_y[s], 1), :]

    pl.semaphore_wait(barrier, ngx - 1 + n_y)
    begin(0, lambda s: px_first.at[s], hx_first, lambda s: py_first.at[s], hy_first)
    if ngy > 1:
        pl.when(gy == 0)(functools.partial(tell, 1))
        pl.when(gy == ngy - 1)(functools.partial(tell, 0))
    both_loaded(2)
    for s in (0, 1):
        e = edge_x[s]
        px_early[s, 0] = slot[e].astype(f32)
        px_early[s, 1] = d[e]
        for x in range(nx):
            py_early[s, pl.ds(x, 1), :] = slot[x, pl.ds(edge_y[s], 1), :].astype(f32)
            py_early[s, pl.ds(nx + x, 1), :] = d[x, pl.ds(edge_y[s], 1), :]
    begin(1, lambda s: px_early.at[s], hx_early, lambda s: py_early.at[s], hy_early)

    for s in (0, 1):

        @pl.when(jnp.logical_not(has_x[s]))
        def _():
            hx_first[s] = jnp.zeros((2, ny, nz), f32)
            hx_early[s] = jnp.zeros((2, ny, nz), f32)
            hx_z[s] = jnp.zeros((ny, nz), f32)

        @pl.when(jnp.logical_not(has_y[s]))
        def _():
            hy_first[s] = jnp.zeros((2 * nx, nz), f32)
            hy_early[s] = jnp.zeros((2 * nx, nz), f32)
            hy_z[s] = jnp.zeros((nx, nz), f32)

    lane = lax.broadcasted_iota(jnp.int32, (ny, nz), 1)
    row = lax.broadcasted_iota(jnp.int32, (ny, nz), 0)
    place = lax.broadcasted_iota(jnp.int32, (HIGH, nz), 0)
    row_half = lax.shift_right_logical(place, 2)
    row_high = 2 * row_half + 4 * jnp.bitwise_and(lax.shift_right_logical(place, 1), 1) + jnp.bitwise_and(place, 1)
    row_low = lax.broadcasted_iota(jnp.int32, (LOW, nz), 0)
    row_wide = lax.broadcasted_iota(jnp.int32, (WIDE, nz), 0)

    def spread(ref, y, rows):
        part = ref[pl.ds(y, 8, stride=0), :]
        return part if rows == 8 else jnp.concatenate([part] * (rows // 8), axis=0)

    def low_rows(slots, y):
        low = jnp.bitwise_and(spread(slots, y, LOW), LOW - 1)
        return jnp.where(low == row_low, 1.0, 0.0).astype(bf16)

    def add_row(sums, slots, fields, right, y):
        mask = lax.shift_right_logical(spread(slots, y, HIGH), 4) == row_high
        left = jnp.concatenate([jnp.where(mask, spread(field, y, HIGH), 0.0) for field in fields], axis=0)
        return sums + lax.dot_general(
            left.astype(bf16), right, (((1,), (1,)), ((), ())), preferred_element_type=f32
        )

    def split(high, low, weighted):
        upper = weighted.astype(bf16).astype(f32)
        high[...] = upper
        low[...] = weighted - upper

    for x in range(nx):
        here = cond[x]
        if x > 0:
            lx[x] = harmonic(cond[x - 1], here)
        right = jnp.where(lane == nz - 1, 0.0, harmonic(here, pltpu.roll(here, nz - 1, 1)))
        up = jnp.where(row == ny - 1, 0.0, harmonic(here, pltpu.roll(here, ny - 1, 0)))
        lz[x] = right
        lzleft[x] = pltpu.roll(right, 1, 1)
        ly[x] = up
        lydown[x] = pltpu.roll(up, 1, 0)
    for x in range(nx):
        phase = m[x]
        cap = jnp.where(phase == 0, 1.0, jnp.where(phase == 1, 2.0, 1.5)).astype(f32)
        whole = cap + lz[x] + lzleft[x] + ly[x] + lydown[x]
        if x > 0:
            whole = whole + lx[x]
        if x < nx - 1:
            whole = whole + lx[x + 1]
        diag[x] = whole

    def apply(field, x):
        v = field[x]
        out = diag[x] * v
        if x > 0:
            out = out - lx[x] * field[x - 1]
        if x < nx - 1:
            out = out - lx[x + 1] * field[x + 1]
        out = out - ly[x] * pltpu.roll(v, ny - 1, 0) - lydown[x] * pltpu.roll(v, 1, 0)
        return out - lz[x] * pltpu.roll(v, nz - 1, 1) - lzleft[x] * pltpu.roll(v, 1, 1)

    for x in range(nx):
        z1[x] = apply(r, x)

    def split_into(x, k, weighted):
        upper = weighted.astype(bf16).astype(f32)
        lower = weighted - upper
        for t in range(nz // SKETCH):
            at = slice(t * SKETCH, (t + 1) * SKETCH)
            parts[x, t, pl.ds(k, ny, stride=4), :] = upper[:, at]
            parts[x, t, pl.ds(k + 1, ny, stride=4), :] = lower[:, at]

    def masked(x, y):
        pair = jnp.concatenate([parts[x, t, pl.ds(y // 2 * 8, 8), :] for t in range(nz // SKETCH)], axis=1)
        swapped = pltpu.roll(pair, 4, 0)
        both = jnp.where(place < 4, pair, swapped) if y % 2 == 0 else jnp.where(place < 4, swapped, pair)
        return jnp.concatenate([both, both], axis=0).astype(bf16) * highs[x, y]

    def matmul(left, right):
        return lax.dot_general(left, right, (((1,), (1,)), ((), ())), preferred_element_type=f32)

    def begin_sketch(x, sums):
        split_into(x, 0, d[x] * r[x])
        split_into(x, 2, jnp.zeros((ny, nz), f32))
        for y in range(ny):
            low = jnp.bitwise_and(spread(slot.at[x], y, WIDE), WIDE - 1)
            right = jnp.where(low == row_wide, 1.0, 0.0).astype(bf16)
            onehot[x, y] = right
            high = lax.shift_right_logical(spread(slot.at[x], y, HIGH), 5)
            mask = [jnp.where(high == row_half + 2 * k, 1.0, 0.0) for k in (0, 1)]
            highs[x, y] = jnp.concatenate(mask, axis=0).astype(bf16)
            sums = sums + matmul(masked(x, y), right)
        return sums

    column = lax.broadcasted_iota(jnp.int32, (HIGH, SKETCH), 1)
    place_row = lax.broadcasted_iota(jnp.int32, (HIGH, SKETCH), 0)

    def padded(block):
        return jnp.concatenate([block, jnp.zeros((HIGH, SKETCH - block.shape[1]), f32)], axis=1)

    def turned(wide, rows, columns):
        wide = pltpu.roll(wide, rows % HIGH, 0) if rows % HIGH else wide
        return pltpu.roll(wide, columns % SKETCH, 1) if columns % SKETCH else wide

    def folded(sums, base, k):
        low, high = padded(sums[:HIGH]), padded(sums[HIGH:])
        low = turned(low + turned(low, -1, 0), -base, 0)
        high = turned(high + turned(high, -1, 0), -base, 0)
        quarter = jnp.bitwise_and(place_row, 3)
        even = turned(jnp.where(quarter == 0, low, turned(high, 2, 0)), 0, k * LOW)
        odd = turned(jnp.where(quarter == 1, turned(low, 1, 0), turned(high, 3, 0)), 0, (k - 1) * LOW)
        out = jnp.where(jnp.bitwise_and(place_row, 1) == 0, even, odd)
        return jnp.where(lax.div(column, LOW) == k, out, 0.0)

    mine[...] = folded(lax.fori_loop(0, nx, begin_sketch, jnp.zeros((2 * HIGH, WIDE), f32)), 0, 3)
    if ngy > 1:
        pl.when(middle)(functools.partial(pass_on, 1))
        pl.when(middle)(functools.partial(pass_on, 0))

    def place_edge(t, rows):
        for y in range(rows):
            onehot_edge[t, y] = low_rows(sedge.at[t], y)

    arrive_beside(near)
    sedge[0] = hx_early[near, 0].astype(jnp.int32)
    place_edge(0, ny)
    arrive(0, hx_first, hy_first)
    for s in (0, 1):
        e = edge_x[s]
        link = harmonic(hx_first[s, 0], cond[e])
        lx[nx * s] = link
        z1[e] = z1[e] + link * (r[e] - hx_first[s, 1])
    for s in (0, 1):
        for x in range(nx):
            here, there = pl.ds(x, 1), pl.ds(nx + x, 1)
            link = harmonic(hy_first[s, there, :], py_first[s, there, :])
            lyb[s, here, :] = link
            flux = link * (py_first[s, here, :] - hy_first[s, here, :])
            after = z1[x, pl.ds(edge_y[s], 1), :] + flux
            z1[x, pl.ds(edge_y[s], 1), :] = after
            py_z[s, here, :] = after
    begin(2, lambda s: z1.at[edge_x[s]], hx_z, lambda s: py_z.at[s], hy_z)
    chains = [jnp.zeros((2 * HIGH, WIDE), f32) for _ in range(2)]

    def sketch_plane(x):
        for y in range(ny):
            chains[y % 2] = chains[y % 2] + matmul(masked(x, y), onehot[x, y])

    for x in range(nx):
        out = apply(z1, x)
        for s in (0, 1):
            if x == edge_x[s]:
                out = out + lx[nx * s] * z1[x]
        z2[x] = out
        for s in (0, 1):
            at = (x, pl.ds(edge_y[s], 1), slice(None))
            z2[at] = z2[at] + lyb[s, pl.ds(x, 1), :] * py_z[s, pl.ds(x, 1), :]
        split_into(x, 0, d[x] * z1[x])
        split_into(x, 2, d[x] * z2[x])
        if x < 2:
            sketch_plane(x)
    edge_chains = [jnp.zeros((2 * HIGH, LOW), f32) for _ in range(2)]

    def sketch_edge(t, rows):
        for y in range(rows):
            edge_chains[y % 2] = add_row(
                edge_chains[y % 2], sedge.at[t], (wedge.at[0, t], wedge.at[1, t]), onehot_edge[t, y], y
            )

    def weigh_face(t, side):
        split(wedge.at[0, t], wedge.at[1, t], -lx[nx * side] * z1[(nx - 1) * side] * hx_early[side, 1])

    weigh_face(0, near)
    sketch_edge(0, ny)
    settle(1, has_y, arrival(1, 1, 0), hy_early, "wait_recv")
    arrive_beside(far)
    for s in (0, 1):
        for x in range(nx):
            at = pl.ds(s * nx + x, 1)
            edge = -lyb[s, pl.ds(x, 1), :] * py_z[s, pl.ds(x, 1), :] * hy_early[s, pl.ds(nx + x, 1), :]
            upper = edge.astype(bf16).astype(f32)
            wedge[0, 1, at, :] = upper
            wedge[1, 1, at, :] = edge - upper
            sedge[1, at, :] = hy_early[s, pl.ds(x, 1), :].astype(jnp.int32)
    place_edge(1, 2 * nx)
    for x in range(2, nx):
        sketch_plane(x)
    sketch_edge(1, 2 * nx)
    sedge[2] = hx_early[far, 0].astype(jnp.int32)
    place_edge(2, ny)
    weigh_face(2, far)
    sketch_edge(2, ny)
    out = mine[...]
    for sums, edge_sums in zip(chains, edge_chains):
        out = out + folded(sums, 0, 1) + folded(sums, 2, 2)
        out = out + padded(edge_sums[:HIGH] + edge_sums[HIGH:])
    mine[...] = out

    def share(step, carry):
        pltpu.make_async_remote_copy(
            src_ref=mine,
            dst_ref=gathered.at[me],
            send_sem=share_sem.at[0],
            recv_sem=share_sem.at[1],
            device_id=peer(step),
            device_id_type=MESH,
        ).start()
        return carry

    for s in (0, 1):

        @pl.when(jnp.logical_and(has_y[1 - s], jnp.logical_not(has_y[s])))
        def _():
            pl.semaphore_wait(known.at[s], 1)

    lax.fori_loop(0, count - 1, share, 0)
    gathered[me] = mine[...]
    arrive(2, hx_z, hy_z)
    for s in (0, 1):
        z2[edge_x[s]] = z2[edge_x[s]] - lx[nx * s] * hx_z[s]
        for x in range(nx):
            at = (x, pl.ds(edge_y[s], 1), slice(None))
            z2[at] = z2[at] - lyb[s, pl.ds(x, 1), :] * hy_z[s, pl.ds(x, 1), :]
    others = gathered.at[pl.ds(0, count - 1)]
    shared = pltpu.make_async_remote_copy(
        src_ref=others,
        dst_ref=others,
        send_sem=share_sem.at[0],
        recv_sem=share_sem.at[1],
        device_id=peer(0),
        device_id_type=MESH,
    )
    shared.wait_recv()
    summed = jnp.sum(gathered[...], axis=0)
    first_lanes = lax.broadcasted_iota(jnp.int32, (HIGH, SKETCH), 1) < LOW
    s0, s1, s2 = (jnp.where(first_lanes, pltpu.roll(summed, SKETCH - k * LOW, 1), 0.0) for k in (3, 1, 2))
    c0, c1 = coefficients(s0, s1, s2 + jnp.where(first_lanes, summed, 0.0))
    for x in range(nx):
        answer[x] = c0 * r[x] + c1 * z1[x]
        rest[x] = r[x] - c0 * z1[x] - c1 * z2[x]
    shared.wait_send()
    settle(0, has_x, sent.at[0], bulk_x, "wait_send")
    settle(1, has_y, sent.at[1], bulk_y, "wait_send")


def put_out(answer, rest, answer_out, rest_out, sem):
    one = pltpu.make_async_copy(answer, answer_out, sem.at[0])
    two = pltpu.make_async_copy(rest, rest_out, sem.at[1])
    one.start()
    two.start()
    one.wait()
    two.wait()


def body(ngx, ngy, f, w, m, s, d):
    nx, ny, nz = f.shape
    count = ngx * ngy
    vm = lambda shape, dtype=f32: pltpu.VMEM(shape, dtype)
    block = (nx, ny, nz)
    assert 2 * nx <= ny and nx % 2 == 0
    answer, rest = pl.pallas_call(
        functools.partial(kernel, ngx, ngy, nx, ny, nz),
        out_shape=(vm(block), vm(block)),
        in_specs=[pl.BlockSpec(memory_space=pl.ANY)] * 5,
        out_specs=[pl.BlockSpec(memory_space=pltpu.VMEM)] * 2,
        scratch_shapes=[
            vm(block), vm(block),
            vm(block), vm(block), vm(block, jnp.int32), vm(block, jnp.int32), vm(block),
            vm(block), vm(block),
            vm((nx + 1, ny, nz)), vm(block), vm(block), vm(block), vm(block), vm((2, nx, nz)),
            vm((nx, ny, WIDE, nz), bf16), vm((nx, ny, 2 * HIGH, nz), bf16), vm((3, ny, LOW, nz), bf16), vm((nx, nz // SKETCH, 4 * ny, SKETCH)), vm((2, 3, ny, nz)), vm((3, ny, nz), jnp.int32),
            vm((2, 2, ny, nz)), vm((2, 2, ny, nz)), vm((2, ny, nz)), vm((2, 2 * nx, nz)), vm((2, 2 * nx, nz)), vm((2, nx, nz)),
            vm((2, 2, ny, nz)), vm((2, 2, ny, nz)), vm((2, 2 * nx, nz)), vm((2, 2 * nx, nz)), vm((2, nx, nz)),
            vm((2, 5, ny, nz)), vm((2, 5, nx, nz)),
            vm((HIGH, SKETCH)), vm((count, HIGH, SKETCH)),
            pltpu.SemaphoreType.DMA((3,)),
            pltpu.SemaphoreType.DMA((2,)),
            pltpu.SemaphoreType.DMA((5,)),
            pltpu.SemaphoreType.DMA((2,)),
            pltpu.SemaphoreType.DMA((2,)),
            pltpu.SemaphoreType.REGULAR((2,)),
        ],
        compiler_params=pltpu.CompilerParams(collective_id=0, has_side_effects=True),
        name="sketched_gmres",
    )(f, w, m, s, d)
    return pl.pallas_call(
        put_out,
        out_shape=(jax.ShapeDtypeStruct(block, f32), jax.ShapeDtypeStruct(block, f32)),
        in_specs=[pl.BlockSpec(memory_space=pltpu.VMEM)] * 2,
        out_specs=[pl.BlockSpec(memory_space=pl.ANY)] * 2,
        scratch_shapes=[pltpu.SemaphoreType.DMA((2,))],
        name="put_out",
    )(pltpu.with_memory_space_constraint(answer, pltpu.VMEM), pltpu.with_memory_space_constraint(rest, pltpu.VMEM))


def solution(mesh):
    spec = P(("parts", "gx"), "gy", None)
    return jax.shard_map(
        functools.partial(body, mesh.shape["gx"], mesh.shape["gy"]),
        mesh=mesh,
        in_specs=(spec,) * 5,
        out_specs=(spec, spec),
        check_vma=False,
    )
```
